32 devices in a mesh: gx: 8 (over y, x, core), gy: 4 (over z).
Axes of the slice: x: 2, y: 2, z: 4, core: 2. Of those that a mesh axis runs over, the one named last changes fastest.
Arguments:
- state_field: float32 [32, 32, 2304], P('gx', 'gy'), may hold values from -6 to 6
- conv_first: float32 [3, 3, 36, 108], replicated, may hold values from -0.1875 to 0.1875
- conv_second: float32 [3, 3, 36, 108], replicated, may hold values from -0.1875 to 0.1875
- spec_real: float32 [32, 32, 36, 432], P('gx', 'gy'), may hold values from -12 to 12
- spec_imag: float32 [32, 32, 36, 432], P('gx', 'gy'), may hold values from -12 to 12
Outputs:
- layer_out: float32 [32, 32, 2304], P('gx', 'gy')
The draws below stay inside these ranges and needn't reach their ends.
All inputs are finite; a program needn't handle non-finite values.
Results may differ from the reference program's by a relative error of at most 0.00007.
Values sent between devices are 32-bit elements; how exact they have to be, the bound alone decides.
No kernel may reach another device: no remote copies, remote signals or barrier semaphores. Data moves between devices by JAX's collectives and lax.ppermute only.
A program may use at most 128 MiB of HBM per device.

```python
import jax
import jax.numpy as jnp
from jax import lax

C = 36
Z = 64
MX = 16
MY = 16
MZ = 12
X = 32
Y = 32


def levels(rng, extent, shards, smallest, largest):
    level, own = 1.0, jax.random.fold_in(rng, 6)
    for dim, parts in shards:
        draws = jnp.exp(jax.random.uniform(jax.random.fold_in(own, dim), (parts,), jnp.float32, smallest / len(shards), largest / len(shards)))
        level = level * jnp.repeat(draws, extent[dim] // parts).reshape([-1 if axis == dim else 1 for axis in range(len(extent))])
    return level


def gaussian(own_key, shape, spread, reach, shards=(), held_as=jnp.bfloat16):
    entries = spread * jax.random.normal(own_key, shape, jnp.float32)
    if shards:
        entries = entries * levels(own_key, shape, shards, -0.22, 0.18)
    return jnp.clip(entries, -reach, reach).astype(held_as)


def setup_inputs(seed: int = 0) -> dict:
    seeds = jax.random.split(jax.random.key(seed), 6)
    state_field = gaussian(seeds[0], (X, Y, C * Z), 1.0, 6.0, ((0, 8), (1, 4)), jnp.float32)
    conv_first = gaussian(seeds[1], (3, 3, C, 3 * C), (27 * C) ** -0.5, 0.1875, (), jnp.float32)
    conv_second = gaussian(seeds[2], (3, 3, C, 3 * C), (27 * C) ** -0.5, 0.1875, (), jnp.float32)
    spec_real = gaussian(seeds[3], (2 * MX, 2 * MY, C, MZ * C), 2.0, 12.0, ((0, 8), (1, 4)), jnp.float32)
    spec_imag = gaussian(seeds[4], (2 * MX, 2 * MY, C, MZ * C), 2.0, 12.0, ((0, 8), (1, 4)), jnp.float32)
    return dict(state_field=state_field, conv_first=conv_first, conv_second=conv_second, spec_real=spec_real, spec_imag=spec_imag)


def kept_modes(mode_count, length):
    places = jnp.arange(2 * mode_count, dtype=jnp.int32)
    return jnp.where(places < mode_count, places, places + length - 2 * mode_count).astype(jnp.int32)


def convolve(volume, kernel):
    operand = jnp.transpose(volume, (2, 0, 1, 3))[None]
    filters = jnp.transpose(kernel.reshape(3, 3, C, 3, C), (2, 4, 0, 1, 3))
    result = lax.conv_general_dilated(operand, filters, (1, 1, 1), [(1, 1), (1, 1), (1, 1)], dimension_numbers=("NCDHW", "OIDHW", "NCDHW"), precision=lax.Precision.HIGHEST)
    return jnp.transpose(result[0], (1, 2, 0, 3))


def reference(state_field, conv_first, conv_second, spec_real, spec_imag):
    highest = lax.Precision.HIGHEST
    volume = state_field.reshape(X, Y, C, Z)
    hidden_field = jax.nn.gelu(convolve(volume, conv_first), approximate=False)
    conv_out = convolve(hidden_field, conv_second)
    coefficients = jnp.fft.rfftn(volume, axes=(0, 1, 3))
    index_x = kept_modes(MX, X)
    index_y = kept_modes(MY, Y)
    picked = coefficients[index_x][:, index_y][:, :, :, :MZ]
    part_real = jnp.real(picked)
    part_imag = jnp.imag(picked)
    weight_real = spec_real.reshape(2 * MX, 2 * MY, C, MZ, C)
    weight_imag = spec_imag.reshape(2 * MX, 2 * MY, C, MZ, C)
    mixed_real = jnp.einsum("abik,abiko->abok", part_real, weight_real, precision=highest) - jnp.einsum("abik,abiko->abok", part_imag, weight_imag, precision=highest)
    mixed_imag = jnp.einsum("abik,abiko->abok", part_real, weight_imag, precision=highest) + jnp.einsum("abik,abiko->abok", part_imag, weight_real, precision=highest)
    full_real = jnp.zeros((X, Y, C, Z // 2 + 1), jnp.float32).at[index_x[:, None], index_y[None, :], :, :MZ].set(mixed_real)
    full_imag = jnp.zeros((X, Y, C, Z // 2 + 1), jnp.float32).at[index_x[:, None], index_y[None, :], :, :MZ].set(mixed_imag)
    spectral = jnp.fft.irfftn(full_real + 1j * full_imag, s=(X, Y, Z), axes=(0, 1, 3))
    layer_out = jax.nn.gelu(spectral + conv_out, approximate=False)
    return layer_out.reshape(X, Y, C * Z)
```

```python
import jax
import jax.numpy as jnp
from jax import lax
from jax.experimental import pallas as pl
from jax.experimental.pallas import tpu as pltpu
from jax.sharding import PartitionSpec as P

C = 36
Z = 64
MX = 16
MY = 16
MZ = 12


BF = jnp.bfloat16
highest = lax.Precision.HIGHEST
two_pi = 6.283185307179586


def with_halo(cells, sides, width):
    for axis, dim in sides:
        count = lax.axis_size(axis)
        ends = count - 1
        head = lax.slice_in_dim(cells, 0, width, axis=dim)
        tail = lax.slice_in_dim(cells, cells.shape[dim] - width, cells.shape[dim], axis=dim)
        cells = jnp.concatenate(
            [
                lax.ppermute(tail, axis, [(i, (i + 1) % count) for i in range(ends)]),
                cells,
                lax.ppermute(head, axis, [((i + 1) % count, i) for i in range(ends)]),
            ],
            axis=dim,
        )
    return cells


def matmul(left, right):
    return jnp.dot(left, right, precision=highest)


def kept_modes(mode_count, length):
    places = jnp.arange(2 * mode_count, dtype=jnp.int32)
    return jnp.where(places < mode_count, places, places + length - 2 * mode_count)


def angle_table(first_index, second_index, length):
    product = first_index[:, None] * second_index[None, :] % length
    angles = product.astype(jnp.float32) * (two_pi / length)
    return (jnp.cos(angles), jnp.sin(angles))


def gelu(x):
    return 0.5*x*(1.0+lax.erf(x*0.7071067811865476))

def split(x):
    hi=x.astype(BF)
    return hi,(x-hi.astype(jnp.float32)).astype(BF)

def conv_body(ext_ref, w1_ref, w2_ref, mask_ref, out_ref, t_ref, d_ref, w_ref, wh_ref, wl_ref):
    f32=jnp.float32
    zb=4
    m=zb*C
    top=40
    rows=Z*C
    d_ref[0:top,:]=jnp.zeros((top,128),f32)
    d_ref[top+rows:,:]=jnp.zeros((d_ref.shape[0]-top-rows,128),f32)
    for j in range(C//2):
        x=ext_ref[:,:,j*128:(j+1)*128].reshape(128,128)
        t_ref[j*128:(j+1)*128,:]=x.T
    for z in range(Z):
        d_ref[top+z*C:top+(z+1)*C,:]=t_ref[pl.ds(z,C,stride=Z),:]
    kk=224
    def load_w(wr):
        w_ref[...]=jnp.zeros_like(w_ref)
        for s in range(9):
            w=wr[s//3,s%3]
            for zo in range(zb):
                w_ref[s*m+zo*C:s*m+(zo+1)*C, 4+C*zo:4+C*zo+3*C]=w
        h,l=split(w_ref[...])
        wh_ref[...]=h
        wl_ref[...]=l
    def conv(store):
        def step(g,_):
            r0=pl.multiple_of(g*2*m,8)
            a=d_ref[pl.ds(r0,kk),:]
            b=d_ref[pl.ds(pl.multiple_of(r0+m,8),kk),:]
            x=jnp.concatenate([a,b],axis=1)
            xh,xl=split(x)
            acc=None
            for s in range(9):
                wh=wh_ref[s*m:(s+1)*m,:]
                wl=wl_ref[s*m:(s+1)*m,:]
                p=jnp.dot(wh,xh,preferred_element_type=f32)+(jnp.dot(wl,xh,preferred_element_type=f32)+jnp.dot(wh,xl,preferred_element_type=f32))
                off=(s//3)*16+s%3
                if off:
                    p=[pltpu.roll(p[:,h*128:(h+1)*128],128-off,1) for h in range(2)]
                else:
                    p=[p[:,h*128:(h+1)*128] for h in range(2)]
                acc=p if acc is None else [u+v for u,v in zip(acc,p)]
            store(r0,acc)
            return 0
        lax.fori_loop(0,Z//(2*zb),step,0)
    load_w(w1_ref)
    mask=mask_ref[0:1,:]
    def store1(r0,acc):
        for h in range(2):
            t_ref[pl.ds(pl.multiple_of(r0+h*m,8),m),:]=gelu(acc[h])*mask
    conv(store1)
    d_ref[top:top+rows,:]=t_ref[...]
    load_w(w2_ref)
    def store2(r0,acc):
        for h in range(2):
            t_ref[pl.ds(pl.multiple_of(r0+h*m,8),m),:]=acc[h]
    conv(store2)
    for j in range(C//2):
        x=jnp.concatenate([t_ref[pl.ds(2*j+e,Z,stride=C),:] for e in range(2)],axis=0)
        y=x.T
        for xx in range(4):
            out_ref[xx,:,j*128:(j+1)*128]=y[16*xx:16*xx+8,:]

def conv_call(ext,w1,w2,mask):
    return pl.pallas_call(conv_body,
        out_shape=jax.ShapeDtypeStruct((4,8,C*Z),jnp.float32),
        in_specs=[pl.BlockSpec(memory_space=pltpu.VMEM)]*4,
        out_specs=pl.BlockSpec(memory_space=pltpu.VMEM),
        scratch_shapes=[pltpu.VMEM((Z*C,128),jnp.float32),pltpu.VMEM((Z*C+80,128),jnp.float32),
            pltpu.VMEM((1296,224),jnp.float32),pltpu.VMEM((1296,224),BF),pltpu.VMEM((1296,224),BF)],
        name="conv_pair",
    )(ext,w1,w2,mask)


def on_device(state_field, conv_first, conv_second, spec_real, spec_imag):
    rows_here = state_field.shape[0]
    cols_here = state_field.shape[1]
    total_x = rows_here * lax.axis_size("gx")
    total_y = cols_here * lax.axis_size("gy")
    row_start = lax.axis_index("gx") * rows_here
    col_start = lax.axis_index("gy") * cols_here
    chan_modes = C * MZ
    width_q = cols_here * chan_modes
    extended = with_halo(state_field, (("gx", 0), ("gy", 1)), 2)
    extended = jnp.pad(extended, ((0, 0), (0, 4), (0, 0)))
    lanes = jnp.arange(128, dtype=jnp.int32)[None, :]
    cell_x = row_start - 1 + lanes // 16
    cell_y = col_start - 1 + lanes % 16
    inside = (cell_x >= 0) & (cell_x < total_x) & (cell_y >= 0) & (cell_y < total_y)
    mask = jnp.broadcast_to(inside.astype(jnp.float32), (8, 128))
    conv_out = conv_call(extended, conv_first, conv_second, mask).reshape(rows_here, cols_here, C, Z)
    z_cells = jnp.arange(Z, dtype=jnp.int32)
    z_freqs = jnp.arange(MZ, dtype=jnp.int32)
    z_cosine, z_sine = angle_table(z_cells, z_freqs, Z)
    flat_cells = state_field.reshape(rows_here * cols_here * C, Z)
    z_real = matmul(flat_cells, z_cosine).reshape(rows_here, width_q)
    z_imag = -matmul(flat_cells, z_sine).reshape(rows_here, width_q)
    x_freqs = kept_modes(MX, total_x)
    local_x = row_start + jnp.arange(rows_here, dtype=jnp.int32)
    frequency = x_freqs
    cosine, sine_part = angle_table(frequency, local_x, total_x)
    term_real = matmul(cosine, z_real) + matmul(sine_part, z_imag)
    term_imag = matmul(cosine, z_imag) - matmul(sine_part, z_real)
    joined = lax.psum_scatter(
        jnp.concatenate([term_real, term_imag], axis=1), "gx", scatter_dimension=0, tiled=True
    )
    mode_real = joined[:, :width_q]
    mode_imag = joined[:, width_q:]
    kxd_rows = mode_real.shape[0]
    y_real = mode_real.reshape(kxd_rows, cols_here, chan_modes)
    y_imag = mode_imag.reshape(kxd_rows, cols_here, chan_modes)
    y_freqs = kept_modes(MY, total_y)
    local_y = col_start + jnp.arange(cols_here, dtype=jnp.int32)
    frequency = y_freqs
    cosine, sine_part = angle_table(frequency, local_y, total_y)
    term_real = jnp.einsum("my,ayq->maq", cosine, y_real, precision=highest) + jnp.einsum(
        "my,ayq->maq", sine_part, y_imag, precision=highest
    )
    term_imag = jnp.einsum("my,ayq->maq", cosine, y_imag, precision=highest) - jnp.einsum(
        "my,ayq->maq", sine_part, y_real, precision=highest
    )
    owned = lax.psum_scatter(
        jnp.concatenate([term_real, term_imag], axis=2), "gy", scatter_dimension=0, tiled=True
    )
    kyd_rows = owned.shape[0]
    owned_real = owned[..., :chan_modes].reshape(kyd_rows, kxd_rows, C, MZ)
    owned_imag = owned[..., chan_modes:].reshape(kyd_rows, kxd_rows, C, MZ)
    weight_real = spec_real.reshape(kxd_rows, kyd_rows, C, MZ, C)
    weight_imag = spec_imag.reshape(kxd_rows, kyd_rows, C, MZ, C)
    mixed_real = jnp.einsum(
        "baik,abiko->baok", owned_real, weight_real, precision=highest
    ) - jnp.einsum("baik,abiko->baok", owned_imag, weight_imag, precision=highest)
    mixed_imag = jnp.einsum(
        "baik,abiko->baok", owned_real, weight_imag, precision=highest
    ) + jnp.einsum("baik,abiko->baok", owned_imag, weight_real, precision=highest)
    mixed = jnp.concatenate(
        [
            mixed_real.reshape(kyd_rows, kxd_rows, chan_modes),
            mixed_imag.reshape(kyd_rows, kxd_rows, chan_modes),
        ],
        axis=2,
    )
    shard_piece = lax.all_gather(mixed, "gy", axis=0, tiled=True)
    frequency = y_freqs
    cosine, sine_part = angle_table(local_y, frequency, total_y)
    piece_real = shard_piece[..., :chan_modes]
    piece_imag = shard_piece[..., chan_modes:]
    add_real = jnp.einsum("ym,maq->ayq", cosine, piece_real, precision=highest) - jnp.einsum(
        "ym,maq->ayq", sine_part, piece_imag, precision=highest
    )
    add_imag = jnp.einsum("ym,maq->ayq", cosine, piece_imag, precision=highest) + jnp.einsum(
        "ym,maq->ayq", sine_part, piece_real, precision=highest
    )
    returned = jnp.concatenate([add_real, add_imag], axis=2)
    back_real = returned[..., :chan_modes].reshape(kxd_rows, width_q)
    back_imag = returned[..., chan_modes:].reshape(kxd_rows, width_q)
    joined_back = jnp.concatenate([back_real, back_imag], axis=1)
    shard_piece = lax.all_gather(joined_back, "gx", axis=0, tiled=True)
    frequency = x_freqs
    cosine, sine_part = angle_table(local_x, frequency, total_x)
    piece_real = shard_piece[:, :width_q]
    piece_imag = shard_piece[:, width_q:]
    add_real = matmul(cosine, piece_real) - matmul(sine_part, piece_imag)
    add_imag = matmul(cosine, piece_imag) + matmul(sine_part, piece_real)
    gathered = jnp.concatenate([add_real, add_imag], axis=1)
    cell_real = gathered[:, :width_q]
    cell_imag = gathered[:, width_q:]
    scaling = 1.0 / (total_x * total_y * Z)
    factors = jnp.where(z_freqs == 0, 1.0, 2.0).astype(jnp.float32) * scaling
    back_cosine, back_sine = angle_table(z_freqs, z_cells, Z)
    back_cosine = back_cosine * factors[:, None]
    back_sine = back_sine * factors[:, None]
    spectral = matmul(cell_real.reshape(rows_here * cols_here * C, MZ), back_cosine) - matmul(
        cell_imag.reshape(rows_here * cols_here * C, MZ), back_sine
    )
    spectral = spectral.reshape(rows_here, cols_here, C, Z)
    layer_out = jax.nn.gelu(spectral + conv_out, approximate=False)
    return layer_out.reshape(rows_here, cols_here, C * Z)


def solution(mesh):
    in_specs = (P("gx", "gy", None), P(), P(), P("gx", "gy", None, None), P("gx", "gy", None, None))
    out_specs = P("gx", "gy", None)
    return jax.shard_map(
        on_device, mesh=mesh, in_specs=in_specs, out_specs=out_specs, check_vma=False
    )
```

```python
import numpy as np
import jax
import jax.numpy as jnp
from jax import lax
from jax.experimental import pallas as pl
from jax.experimental.pallas import tpu as pltpu
from jax.sharding import PartitionSpec as P

C = 36
Z = 64
MX = 16
MY = 16
MZ = 12
BF = jnp.bfloat16
highest = lax.Precision.HIGHEST


def with_halo(cells, sides, width):
    for axis, dim in sides:
        count = lax.axis_size(axis)
        ends = count - 1
        head = lax.slice_in_dim(cells, 0, width, axis=dim)
        tail = lax.slice_in_dim(cells, cells.shape[dim] - width, cells.shape[dim], axis=dim)
        cells = jnp.concatenate(
            [
                lax.ppermute(tail, axis, [(i, (i + 1) % count) for i in range(ends)]),
                cells,
                lax.ppermute(head, axis, [((i + 1) % count, i) for i in range(ends)]),
            ],
            axis=dim,
        )
    return cells


def gelu(x):
    return 0.5*x*(1.0+lax.erf(x*0.7071067811865476))

def split(x):
    hi=x.astype(BF)
    return hi,(x-hi.astype(jnp.float32)).astype(BF)

def conv_body(ext_ref, w1_ref, w2_ref, mask_ref, out_ref, t_ref, d_ref, w_ref, wh_ref, wl_ref):
    f32=jnp.float32
    zb=4
    m=zb*C
    top=40
    rows=Z*C
    d_ref[0:top,:]=jnp.zeros((top,128),f32)
    d_ref[top+rows:,:]=jnp.zeros((d_ref.shape[0]-top-rows,128),f32)
    for j in range(C//2):
        x=ext_ref[:,:,j*128:(j+1)*128].reshape(128,128)
        t_ref[j*128:(j+1)*128,:]=x.T
    for z in range(Z):
        d_ref[top+z*C:top+(z+1)*C,:]=t_ref[pl.ds(z,C,stride=Z),:]
    kk=224
    def load_w(wr):
        w_ref[...]=jnp.zeros_like(w_ref)
        for s in range(9):
            w=wr[s//3,s%3]
            for zo in range(zb):
                w_ref[s*m+zo*C:s*m+(zo+1)*C, 4+C*zo:4+C*zo+3*C]=w
        h,l=split(w_ref[...])
        wh_ref[...]=h
        wl_ref[...]=l
    def conv(store):
        def step(g,_):
            r0=pl.multiple_of(g*2*m,8)
            a=d_ref[pl.ds(r0,kk),:]
            b=d_ref[pl.ds(pl.multiple_of(r0+m,8),kk),:]
            x=jnp.concatenate([a,b],axis=1)
            xh,xl=split(x)
            acc=None
            for s in range(9):
                wh=wh_ref[s*m:(s+1)*m,:]
                wl=wl_ref[s*m:(s+1)*m,:]
                p=jnp.dot(wh,xh,preferred_element_type=f32)+(jnp.dot(wl,xh,preferred_element_type=f32)+jnp.dot(wh,xl,preferred_element_type=f32))
                off=(s//3)*16+s%3
                if off:
                    p=[pltpu.roll(p[:,h*128:(h+1)*128],128-off,1) for h in range(2)]
                else:
                    p=[p[:,h*128:(h+1)*128] for h in range(2)]
                acc=p if acc is None else [u+v for u,v in zip(acc,p)]
            store(r0,acc)
            return 0
        lax.fori_loop(0,Z//(2*zb),step,0)
    load_w(w1_ref)
    mask=mask_ref[0:1,:]
    def store1(r0,acc):
        for h in range(2):
            t_ref[pl.ds(pl.multiple_of(r0+h*m,8),m),:]=gelu(acc[h])*mask
    conv(store1)
    d_ref[top:top+rows,:]=t_ref[...]
    load_w(w2_ref)
    def store2(r0,acc):
        for h in range(2):
            t_ref[pl.ds(pl.multiple_of(r0+h*m,8),m),:]=acc[h]
    conv(store2)
    for j in range(C//2):
        x=jnp.concatenate([t_ref[pl.ds(2*j+e,Z,stride=C),:] for e in range(2)],axis=0)
        y=x.T
        for xx in range(4):
            out_ref[xx,:,j*128:(j+1)*128]=y[16*xx:16*xx+8,:]

def conv_call(ext,w1,w2,mask):
    return pl.pallas_call(conv_body,
        out_shape=jax.ShapeDtypeStruct((4,8,C*Z),jnp.float32),
        in_specs=[pl.BlockSpec(memory_space=pltpu.VMEM)]*4,
        out_specs=pl.BlockSpec(memory_space=pltpu.VMEM),
        scratch_shapes=[pltpu.VMEM((Z*C,128),jnp.float32),pltpu.VMEM((Z*C+80,128),jnp.float32),
            pltpu.VMEM((1296,224),jnp.float32),pltpu.VMEM((1296,224),BF),pltpu.VMEM((1296,224),BF)],
        name="conv_pair",
    )(ext,w1,w2,mask)


def dft_wave(freqs, length, sign):
    angle = sign * 2.0 * np.pi * np.outer(freqs, np.arange(length)) / length
    return np.cos(angle) + 1j * np.sin(angle)


def mode_freqs(kept, length):
    places = np.arange(2 * kept)
    return np.where(places < kept, places, places + length - 2 * kept)


def line_table(wave, outer, inner, outer_to, inner_to):
    shaped = wave.reshape(outer_to, inner_to, outer, inner)
    parts = np.stack([shaped.real, shaped.imag])
    table = np.einsum("cbqal,jk->lajcqbk", parts, np.eye(4))
    return table.reshape(inner * outer * 4, 2 * inner_to * outer_to * 4).astype(np.float32)


def plane_table(wave, outer, inner, outer_to, inner_to, order):
    shaped = wave.reshape(outer_to, inner_to, outer, inner)
    turned = np.stack([np.stack([shaped * 1j ** (c + r) for r in range(2)]) for c in range(2)])
    parts = np.stack([turned.real, turned.imag])
    table = np.einsum("ecrpmal->" + order + "carl", parts)
    return table.reshape(2 * outer_to * inner_to, 4 * outer * inner).astype(np.float32)


def dot(left, right):
    return jnp.dot(left, right, precision=highest, preferred_element_type=jnp.float32)


def swap_lanes(tiles, low):
    tiles = list(tiles)
    lane = lax.broadcasted_iota(jnp.int32, (8, 128), 1)
    bit = 1
    while bit < len(tiles):
        width = low * bit
        upper = (lane & width) != 0
        for at in range(len(tiles)):
            if at & bit == 0:
                first, second = tiles[at], tiles[at | bit]
                tiles[at] = jnp.where(upper, pltpu.roll(second, width, 1), first)
                tiles[at | bit] = jnp.where(upper, second, pltpu.roll(first, 128 - width, 1))
        bit *= 2
    return tiles


def swap_halves(tile):
    row = lax.broadcasted_iota(jnp.int32, (8, 128), 0)
    lane = lax.broadcasted_iota(jnp.int32, (8, 128), 1)
    same = (row >= 4) == (lane >= 64)
    return jnp.where(same, tile, pltpu.roll(pltpu.roll(tile, 4, 0), 64, 1))


def forward_z_body(cells_ref, table_ref, out_ref, rows_ref):
    groups = C // 4
    stacked = jnp.concatenate(
        [cells_ref[:, :, g * 256 : (g + 1) * 256].reshape(32, 256) for g in range(groups)], axis=0
    )
    rows_ref[0 : 32 * groups, :] = dot(stacked, table_ref[...])
    rows_ref[32 * groups :, :] = jnp.zeros((32, 128), jnp.float32)
    for pair in range((groups + 1) // 2):
        tiles = [
            swap_halves(rows_ref[pl.ds(64 * pair + y, 8, stride=8), :]) for y in range(8)
        ]
        tiles = swap_lanes(tiles, 16)
        for slot in range(8):
            group, part = 2 * pair + slot // 4, slot % 4
            if group < groups and part < 3:
                out_ref[group * 3 + part] = tiles[slot]
    for spare in range(3 * groups, out_ref.shape[0]):
        out_ref[spare] = jnp.zeros((8, 128), jnp.float32)


def planes(in_ref, line_ref, plane_ref, rows_ref, outer, inner):
    for a in range(outer):
        tiles = swap_lanes([in_ref[a * inner + b] for b in range(inner)], 4)
        for k in range(4):
            rows_ref[k * 8 * outer + a * 8 : k * 8 * outer + a * 8 + 8, :] = tiles[k]
    lines = dot(rows_ref[...], line_ref[...])
    results = []
    for k in range(4):
        part = lines[k * 8 * outer : (k + 1) * 8 * outer]
        stacked = jnp.concatenate([part[:, :128], part[:, 128:]], axis=0)
        results.append(dot(plane_ref[...], stacked))
    return results


def forward_xy_body(in_ref, line_ref, plane_ref, out_ref, rows_ref, turn_ref):
    outer, inner = 8, 4
    results = planes(in_ref, line_ref, plane_ref, rows_ref, outer, inner)
    for k in range(4):
        turn_ref[pl.ds(k, 8 * outer, stride=4), :] = results[k]
    for a in range(outer):
        tiles = swap_lanes([turn_ref[a * 32 + m * 8 : a * 32 + m * 8 + 8, :] for m in range(4)], 4)
        for b in range(inner):
            out_ref[a * inner + b] = tiles[b]


def inverse_xy_body(in_ref, line_ref, plane_ref, out_ref, rows_ref):
    outer, inner = 8, 4
    results = planes(in_ref, line_ref, plane_ref, rows_ref, outer, inner)
    for a in range(outer):
        tiles = swap_lanes([results[k][a * 8 : a * 8 + 8] for k in range(4)], 4)
        for b in range(inner):
            out_ref[a * inner + b] = tiles[b]


def mix_body(in_ref, real_ref, imag_ref, spread_ref, order_ref, out_ref, left_ref, mixed_ref):
    groups = C // 4
    pairs = (groups + 1) // 2
    row = lax.broadcasted_iota(jnp.int32, (8, 128), 0)
    low = row < 4
    zero = jnp.zeros((8, 128), jnp.float32)
    for t in range(pairs):
        real_parts, imag_parts = [], []
        for part in range(3):
            first = in_ref[2 * t * 3 + part]
            second = in_ref[(2 * t + 1) * 3 + part] if 2 * t + 1 < groups else zero
            real_parts.append(jnp.where(low, first, pltpu.roll(second, 4, 0)))
            imag_parts.append(jnp.where(low, pltpu.roll(first, 4, 0), second))
        for e, parts in enumerate((real_parts, imag_parts)):
            tiles = swap_lanes(parts + [zero], 4)
            for m in range(4):
                at = ((e * 4 + m) * pairs + t) * 8
                left_ref[at : at + 8, :] = tiles[m]
    hi, lo = split(left_ref[...])
    left = jnp.concatenate([hi, lo], axis=1)

    def step(q, carry):
        table = spread_ref[q]
        spread = jnp.dot(
            left, jnp.concatenate([table, table], axis=0), preferred_element_type=jnp.float32
        )
        for m in range(4):
            re = spread[m * 8 * pairs : m * 8 * pairs + C]
            im = spread[(4 + m) * 8 * pairs : (4 + m) * 8 * pairs + C]
            wr = real_ref[m, q]
            wi = imag_ref[m, q]
            at = q * 8 + m
            mixed_ref[pl.ds(at, 1), :] = jnp.sum(re * wr - im * wi, axis=0, keepdims=True)
            mixed_ref[pl.ds(at + 4, 1), :] = jnp.sum(re * wi + im * wr, axis=0, keepdims=True)
        return carry

    lax.fori_loop(0, 8, step, 0)
    mixed = mixed_ref[...]
    hi = mixed.astype(BF)
    rest = mixed - hi.astype(jnp.float32)
    mid, lo = split(rest)
    placed = jnp.dot(
        jnp.concatenate([hi, mid, lo], axis=0), order_ref[...], preferred_element_type=jnp.float32
    )
    placed = placed[0:64] + (placed[64:128] + placed[128:192])
    for block in range(out_ref.shape[0] // 8):
        tiles = [placed[8 * q : 8 * q + 8, block * 128 : (block + 1) * 128] for q in range(8)]
        tiles = swap_lanes(tiles, 16)
        for slot in range(8):
            out_ref[block * 8 + slot] = tiles[slot]


def inverse_z_body(in_ref, table_ref, conv_ref, out_ref, rows_ref, cells_ref):
    groups = C // 4
    zero = jnp.zeros((8, 128), jnp.float32)
    pairs = (groups + 1) // 2
    for pair in range(pairs):
        tiles = []
        for slot in range(8):
            group, part = 2 * pair + slot // 4, slot % 4
            tiles.append(in_ref[group * 3 + part] if group < groups and part < 3 else zero)
        tiles = swap_lanes(tiles, 16)
        for y in range(8):
            rows_ref[64 * pair + 8 * y : 64 * pair + 8 * y + 8, :] = swap_halves(tiles[y])
    for half in range(2):
        cells_ref[half] = dot(rows_ref[...], table_ref[:, half * 128 : (half + 1) * 128])
    for x in range(4):
        for group in range(groups):
            at = 64 * (group // 2) + 4 * (group % 2) + x
            for half in range(2):
                lanes = slice(group * 256 + half * 128, group * 256 + half * 128 + 128)
                spectral = cells_ref[half, pl.ds(at, 8, stride=8), :]
                out_ref[x, :, lanes] = gelu(spectral + conv_ref[x, :, lanes])


def local_call(body, out_shape, scratch, name, *operands):
    return pl.pallas_call(
        body,
        out_shape=jax.ShapeDtypeStruct(out_shape, jnp.float32),
        in_specs=[pl.BlockSpec(memory_space=pltpu.VMEM)] * len(operands),
        out_specs=pl.BlockSpec(memory_space=pltpu.VMEM),
        scratch_shapes=scratch,
        name=name,
    )(*operands)


def complex_product(spec, table, real, imag):
    cosine = jnp.asarray(table.real.astype(np.float32))
    sine = jnp.asarray(table.imag.astype(np.float32))

    def product(left, right):
        return jnp.einsum(spec, left, right, precision=highest)

    return (
        product(cosine, real) - product(sine, imag),
        product(cosine, imag) + product(sine, real),
    )


def transform(wave_x, wave_y, parts, split_to):
    a, b, _, x, y, _, _ = parts.shape
    shaped = jnp.transpose(parts, (2, 0, 3, 1, 4, 5, 6)).reshape(2, a * x, b * y, 4, 4)
    real, imag = complex_product("qy,xykj->xqkj", wave_y, shaped[0], shaped[1])
    real, imag = complex_product("px,xqkj->pqkj", wave_x, real, imag)
    return jnp.stack([real, imag]).reshape((2,) + split_to + (4, 4))


def on_device(state_field, conv_first, conv_second, spec_real, spec_imag):
    rows_here, cols_here = state_field.shape[:2]
    kept_x, kept_y = spec_real.shape[:2]
    count_x, count_y = lax.axis_size("gx"), lax.axis_size("gy")
    devices = count_x * count_y
    total_x, total_y = rows_here * count_x, cols_here * count_y
    groups, thirds = C // 4, MZ // 4
    owners = groups * thirds
    if (rows_here, cols_here) != (4, 8) or owners > devices:
        raise ValueError("unsupported block")
    both = ("gx", "gy")
    row_start = lax.axis_index("gx") * rows_here
    col_start = lax.axis_index("gy") * cols_here
    f32 = jnp.float32

    wave_z = dft_wave(np.arange(MZ), Z, -1.0).reshape(thirds, 4, Z)
    wave_z = np.concatenate([wave_z, np.zeros((1, 4, Z))])
    parts_z = np.stack([wave_z.real, wave_z.imag])
    forward_z = np.einsum("egrz,ck->czegkr", parts_z, np.eye(4)).reshape(4 * Z, 128)
    gains = np.where(np.arange(16) == 0, 1.0, 2.0).reshape(4, 4) / (total_x * total_y * Z)
    inverse_z = np.einsum("egrz,gr,ck->egcrkz", parts_z, gains, np.eye(4)).reshape(128, 4 * Z)
    forward_x = dft_wave(mode_freqs(MX, total_x), total_x, -1.0)
    forward_y = dft_wave(mode_freqs(MY, total_y), total_y, -1.0)
    inverse_x, inverse_y = np.conj(forward_x).T, np.conj(forward_y).T

    extended = with_halo(state_field, (("gx", 0), ("gy", 1)), 2)
    extended = jnp.pad(extended, ((0, 0), (0, 4), (0, 0)))
    lanes = jnp.arange(128, dtype=jnp.int32)[None, :]
    cell_x = row_start - 1 + lanes // 16
    cell_y = col_start - 1 + lanes % 16
    inside = (cell_x >= 0) & (cell_x < total_x) & (cell_y >= 0) & (cell_y < total_y)
    mask = jnp.broadcast_to(inside.astype(f32), (8, 128))
    conv_out = conv_call(extended, conv_first, conv_second, mask)

    columns = local_call(
        forward_z_body,
        (devices, 8, 128),
        [pltpu.VMEM((32 * (groups + 1), 128), f32)],
        "forward_z",
        state_field,
        jnp.asarray(forward_z.astype(np.float32)),
    )
    columns = lax.all_to_all(columns, both, 0, 0, tiled=True)
    fast = (count_x, count_y, kept_x, kept_y) == (8, 4, 4, 8)
    if fast:
        pairs = (groups + 1) // 2
        modes = local_call(
            forward_xy_body,
            (devices, 8, 128),
            [pltpu.VMEM((256, 128), f32)] * 2,
            "forward_xy",
            columns,
            line_table(forward_y, count_y, cols_here, count_y, kept_y),
            plane_table(forward_x, count_x, rows_here, count_x, kept_x, "pme"),
        )
        modes = lax.all_to_all(modes, both, 0, 0, tiled=True)
        spread = np.zeros((kept_y, kept_y, 16, MZ, C))
        for q in range(kept_y):
            for r in range(MZ):
                spread[q, q, r, r, :] = 1.0
        order = np.zeros((MZ, C, devices, 16))
        for r in range(MZ):
            for o in range(C):
                order[r, o, (o // 4) * thirds + r // 4, (o % 4) * 4 + r % 4] = 1.0
        mixed = local_call(
            mix_body,
            (devices, 8, 128),
            [pltpu.VMEM((2 * 4 * pairs * 8, 128), f32), pltpu.VMEM((64, MZ * C), f32)],
            "mix",
            modes,
            spec_real,
            spec_imag,
            jnp.asarray(spread.reshape(kept_y, 128, MZ * C), BF),
            jnp.asarray(order.reshape(MZ * C, devices * 16), BF),
        )
        mixed = lax.all_to_all(mixed, both, 0, 0, tiled=True)
        back = local_call(
            inverse_xy_body,
            (devices, 8, 128),
            [pltpu.VMEM((256, 128), f32)],
            "inverse_xy",
            mixed,
            line_table(inverse_y, count_y, kept_y, count_y, cols_here),
            plane_table(inverse_x, count_x, kept_x, count_x, rows_here, "pem"),
        )
    else:
        parts = columns.reshape(count_x, count_y, 2, rows_here, cols_here, 4, 4)
        modes = transform(
            forward_x, forward_y, parts, (count_x, kept_x, count_y, kept_y)
        )
        modes = jnp.transpose(modes, (1, 3, 0, 5, 4, 2, 6))
        modes = modes.reshape(devices, 8, kept_y * kept_x * 4)
        modes = lax.all_to_all(modes, both, 0, 0, tiled=True)[:owners]
        modes = modes.reshape(groups, thirds, 2, 4, kept_y, kept_x, 4)
        modes = jnp.transpose(modes, (2, 5, 4, 0, 3, 1, 6))
        modes = modes.reshape(2, kept_x, kept_y, C, MZ)
        weight_real = spec_real.reshape(kept_x, kept_y, C, MZ, C)
        weight_imag = spec_imag.reshape(kept_x, kept_y, C, MZ, C)

        def product(left, right):
            return jnp.einsum("abik,abiko->abok", left, right, precision=highest)

        mixed = jnp.stack(
            [
                product(modes[0], weight_real) - product(modes[1], weight_imag),
                product(modes[0], weight_imag) + product(modes[1], weight_real),
            ]
        ).reshape(2, kept_x, kept_y, groups, 4, thirds, 4)
        mixed = jnp.transpose(mixed, (3, 5, 0, 1, 2, 4, 6))
        mixed = mixed.reshape(owners, 2 * kept_x, kept_y * 16)
        mixed = jnp.pad(mixed, ((0, devices - owners), (0, 0), (0, 0)))
        mixed = lax.all_to_all(mixed, both, 0, 0, tiled=True)
        parts = mixed.reshape(count_x, count_y, 2, kept_x, kept_y, 4, 4)
        back = transform(
            inverse_x, inverse_y, parts, (count_x, rows_here, count_y, cols_here)
        )
        back = jnp.transpose(back, (1, 3, 0, 2, 4, 5, 6)).reshape(devices, 8, 128)
    back = lax.all_to_all(back, both, 0, 0, tiled=True)
    return local_call(
        inverse_z_body,
        (rows_here, cols_here, C * Z),
        [pltpu.VMEM((64 * ((groups + 1) // 2), 128), f32), pltpu.VMEM((2, 64 * ((groups + 1) // 2), 128), f32)],
        "inverse_z",
        back,
        jnp.asarray(inverse_z.astype(np.float32)),
        conv_out,
    )


def solution(mesh):
    in_specs = (P("gx", "gy", None), P(), P(), P("gx", "gy", None, None), P("gx", "gy", None, None))
    out_specs = P("gx", "gy", None)
    return jax.shard_map(
        on_device, mesh=mesh, in_specs=in_specs, out_specs=out_specs, check_vma=False
    )
```

```python
import numpy as np
import jax
import jax.numpy as jnp
from jax import lax
from jax.experimental import pallas as pl
from jax.experimental.pallas import tpu as pltpu
from jax.sharding import PartitionSpec as P


C = 36
Z = 64
MX = 16
MY = 16
MZ = 12
BF = jnp.bfloat16
highest = lax.Precision.HIGHEST


def gelu(x):
    return 0.5 * x * (1.0 + lax.erf(x * 0.7071067811865476))


def split(x):
    hi = x.astype(BF)
    return hi, (x - hi.astype(jnp.float32)).astype(BF)


STEP = 4
TOP = 40
DEPTH = 224
ROWS = Z * C
BLOCK = STEP * C


def load_filters(filter_ref, wide_ref, hi_ref, lo_ref):
    wide_ref[...] = jnp.zeros_like(wide_ref)
    for s in range(9):
        taps = filter_ref[s // 3, s % 3]
        for z in range(STEP):
            at = s * BLOCK + z * C
            lane = TOP - C + C * z
            wide_ref[at : at + C, lane : lane + 3 * C] = taps
    hi_ref[...], lo_ref[...] = split(wide_ref[...])


def convolve(data_ref, hi_ref, lo_ref, store):
    f32 = jnp.float32

    def step(g, carry):
        at = pl.multiple_of(g * 2 * BLOCK, 8)
        window = jnp.concatenate(
            [data_ref[pl.ds(pl.multiple_of(at + h * BLOCK, 8), DEPTH), :] for h in range(2)], axis=1
        )
        data_hi, data_lo = split(window)
        total = None
        for s in range(9):
            hi = hi_ref[s * BLOCK : (s + 1) * BLOCK, :]
            lo = lo_ref[s * BLOCK : (s + 1) * BLOCK, :]
            part = jnp.dot(hi, data_hi, preferred_element_type=f32) + (
                jnp.dot(lo, data_hi, preferred_element_type=f32)
                + jnp.dot(hi, data_lo, preferred_element_type=f32)
            )
            halves = [part[:, :128], part[:, 128:]]
            shift = (s // 3 - 1) * 16 + s % 3 - 1
            if shift:
                halves = [pltpu.roll(half, -shift % 128, 1) for half in halves]
            total = halves if total is None else [u + v for u, v in zip(total, halves)]
        for h in range(2):
            store(pl.multiple_of(at + h * BLOCK, 8), total[h])
        return carry

    lax.fori_loop(0, Z // (2 * STEP), step, 0)


def first_conv_body(
    cells_ref, top_ref, bottom_ref, left_ref, right_ref, filter_ref, mask_ref,
    out_ref, frame_ref, turn_ref, data_ref, wide_ref, hi_ref, lo_ref,
):
    f32 = jnp.float32
    frame_ref[:, 8:16, :] = jnp.zeros((8, 8, C * Z), f32)
    frame_ref[0:2, 0:8, :] = top_ref[...]
    frame_ref[2:6, 0:8, :] = cells_ref[...]
    frame_ref[6:8, 0:8, :] = bottom_ref[...]
    for x in range(8):
        frame_ref[x, 8:10, :] = right_ref[x]
        frame_ref[(x + 7) % 8, 14:16, :] = left_ref[x]
    data_ref[0:TOP, :] = jnp.zeros((TOP, 128), f32)
    data_ref[TOP + ROWS :, :] = jnp.zeros((TOP, 128), f32)
    for j in range(C * Z // 128):
        lanes = slice(j * 128, (j + 1) * 128)
        turn_ref[lanes, :] = frame_ref[:, :, lanes].reshape(128, 128).T
    for z in range(Z):
        data_ref[TOP + z * C : TOP + (z + 1) * C, :] = turn_ref[pl.ds(z, C, stride=Z), :]
    load_filters(filter_ref, wide_ref, hi_ref, lo_ref)
    mask = mask_ref[0:1, :]

    def store(at, total):
        turn_ref[pl.ds(at, BLOCK), :] = gelu(total) * mask

    convolve(data_ref, hi_ref, lo_ref, store)
    out_ref[0:TOP, :] = jnp.zeros((TOP, 128), f32)
    out_ref[TOP + ROWS :, :] = jnp.zeros((TOP, 128), f32)
    out_ref[TOP : TOP + ROWS, :] = turn_ref[...]


def second_conv_body(data_ref, filter_ref, out_ref, turn_ref, wide_ref, hi_ref, lo_ref):
    load_filters(filter_ref, wide_ref, hi_ref, lo_ref)

    def store(at, total):
        turn_ref[pl.ds(at, BLOCK), :] = total

    convolve(data_ref, hi_ref, lo_ref, store)
    for j in range(C * Z // 128):
        pieces = [turn_ref[pl.ds(2 * j + e, Z, stride=C), :] for e in range(2)]
        turned = jnp.concatenate(pieces, axis=0).T
        for x in range(4):
            out_ref[x, :, j * 128 : (j + 1) * 128] = turned[16 * x + 32 : 16 * x + 40, :]


def dft_wave(freqs, length, sign):
    angle = sign * 2.0 * np.pi * np.outer(freqs, np.arange(length)) / length
    return np.cos(angle) + 1j * np.sin(angle)


def mode_freqs(kept, length):
    places = np.arange(2 * kept)
    return np.where(places < kept, places, places + length - 2 * kept)


def halves(table):
    hi = table.astype(BF)
    lo = (table - hi.astype(np.float64)).astype(BF)
    return hi, lo


def line_table(wave, outer_to, inner_to, outer, inner):
    shaped = wave.reshape(outer_to, inner_to, outer, inner)
    turned = np.stack([shaped, shaped * 1j])
    parts = np.stack([turned.real, turned.imag])
    table = np.einsum("crAmal,uv->rlaucmAv", parts, np.eye(2))
    return table.reshape(4 * inner * outer, 4 * inner_to * outer_to)


def plane_table(lines, wave):
    cross = np.concatenate([wave.real, wave.imag])
    cross = np.pad(cross, ((0, 0), (0, lines.shape[1] - cross.shape[1])))
    return np.stack(halves(np.concatenate([lines, cross])))


def dot(left, right_hi, right_lo):
    f32 = jnp.float32
    hi, lo = split(left)
    return jnp.dot(hi, right_hi, preferred_element_type=f32) + (
        jnp.dot(lo, right_hi, preferred_element_type=f32)
        + jnp.dot(hi, right_lo, preferred_element_type=f32)
    )


def swap_lanes(tiles, low):
    tiles = list(tiles)
    lane = lax.broadcasted_iota(jnp.int32, (8, 128), 1)
    bit = 1
    while bit < len(tiles):
        width = low * bit
        upper = (lane & width) != 0
        for at in range(len(tiles)):
            if at & bit == 0:
                first, second = tiles[at], tiles[at | bit]
                tiles[at] = jnp.where(upper, pltpu.roll(second, width, 1), first)
                tiles[at | bit] = jnp.where(upper, second, pltpu.roll(first, 128 - width, 1))
        bit *= 2
    return tiles


def forward_z_body(field_ref, waves_ref, out_ref, head_ref, tail_ref, cells_ref, table_ref, sems):
    groups = C // 4
    copies = [
        pltpu.make_async_copy(field_ref, cells_ref, sems.at[0]),
        pltpu.make_async_copy(waves_ref, table_ref, sems.at[1]),
    ]
    for copy in copies:
        copy.start()
    for copy in copies:
        copy.wait()
    rows = cells_ref.shape[0]
    head_ref[...] = cells_ref[0:2]
    tail_ref[...] = cells_ref[rows - 2 : rows]
    stacked = jnp.concatenate(
        [cells_ref[:, :, g * 256 : (g + 1) * 256].reshape(32, 256) for g in range(groups)], axis=0
    )
    waves = dot(stacked, table_ref[0], table_ref[1])
    for group in range(groups):
        at = 32 * group
        tiles = swap_lanes([waves[at + 8 * x : at + 8 * x + 8] for x in range(4)], 16)
        for part in range(3):
            out_ref[group * 3 + part] = tiles[part]
    for spare in range(3 * groups, out_ref.shape[0]):
        out_ref[spare] = jnp.zeros((8, 128), jnp.float32)


def plane_body(in_ref, table_ref, out_ref, rows_ref):
    f32 = jnp.float32
    outer, inner = 8, 4
    for b in range(inner):
        tiles = swap_lanes([in_ref[a * inner + b] for a in range(outer)], 2)
        for g in range(8):
            rows_ref[g * 32 + b * 8 : g * 32 + b * 8 + 8, :] = tiles[g]
    lines = dot(rows_ref[...], table_ref[0, 0:128, :], table_ref[1, 0:128, :])
    minus = lax.broadcasted_iota(jnp.int32, (32, 128), 1) < 64
    results = []
    cross_hi, cross_lo = table_ref[0, 128:192, 0:32], table_ref[1, 128:192, 0:32]
    for g in range(0, 8, 2):
        part = jnp.concatenate([lines[g * 32 : g * 32 + 32], lines[g * 32 + 32 : g * 32 + 64]], axis=1)
        hi, lo = split(part)
        both = jnp.dot(cross_hi, hi, preferred_element_type=f32) + (
            jnp.dot(cross_lo, hi, preferred_element_type=f32)
            + jnp.dot(cross_hi, lo, preferred_element_type=f32)
        )
        for h in range(2):
            turned = pltpu.roll(both[32:, h * 128 : h * 128 + 128], 64, 1)
            plain = both[:32, h * 128 : h * 128 + 128]
            results.append(jnp.where(minus, plain - turned, plain + turned))
    for b in range(inner):
        tiles = swap_lanes([results[g][b * 8 : b * 8 + 8] for g in range(8)], 2)
        for a in range(outer):
            out_ref[a * inner + b] = tiles[a]


def mode_of(place):
    return jnp.floor((place.astype(jnp.float32) + 0.5) * (1.0 / C)).astype(jnp.int32)


def mix_body(in_ref, real_hbm, imag_hbm, out_ref, left_ref, real_ref, imag_ref, sems):
    f32 = jnp.float32
    groups = C // 4
    copies = [
        [
            pltpu.make_async_copy(source.at[:, :, k], held.at[k], sems.at[k, e])
            for e, (source, held) in enumerate(((real_hbm, real_ref), (imag_hbm, imag_ref)))
        ]
        for k in range(4)
    ]
    for pair in copies:
        for copy in pair:
            copy.start()
    width = MZ * C
    lane = lax.broadcasted_iota(jnp.int32, (256, width), 0) & 127
    mode = mode_of(lax.broadcasted_iota(jnp.int32, (1, width), 1))
    wanted = lane - ((mode >> 2) * 16 + (mode & 3))
    place = lax.broadcasted_iota(jnp.int32, (width, 1), 0)
    mode = mode_of(place)
    channel = place - mode * C
    column = ((channel >> 2) * 3 + (mode >> 2)) * 16 + (channel & 3) * 4 + (mode & 3)
    slots = lax.broadcasted_iota(jnp.int32, (width, out_ref.shape[0] * 16), 1)
    order = jnp.where(slots == column, 1.0, 0.0).astype(BF)
    zero = jnp.zeros((8, 128), f32)
    for group in range(groups):
        tiles = swap_lanes([in_ref[group * 3 + part] for part in range(3)] + [zero], 16)
        for m in range(4):
            at = (m * groups + group) * 8
            left_ref[at : at + 8, :] = tiles[m]
    hi, lo = split(left_ref[...])
    left = jnp.concatenate([hi, lo], axis=1)
    real = [jnp.zeros((8, MZ * C), f32) for _ in range(4)]
    imag = [jnp.zeros((8, MZ * C), f32) for _ in range(4)]
    for k in range(4):
        sides = []
        for e in range(2):
            table = jnp.where(wanted == e * 64 + k * 4, 1.0, 0.0).astype(BF)
            sides.append(jnp.dot(left, table, preferred_element_type=f32))
        for copy in copies[k]:
            copy.wait()
        for m in range(4):
            for group in range(groups):
                at = (m * groups + group) * 8
                re = sides[0][at : at + 8]
                im = sides[1][at : at + 8]
                wr = real_ref[k, m, group]
                wi = imag_ref[k, m, group]
                real[m] = real[m] + (re * wr - im * wi)
                imag[m] = imag[m] + (re * wi + im * wr)
    hi, lo = split(jnp.concatenate(real + imag, axis=0))
    placed = jnp.dot(jnp.concatenate([hi, lo], axis=0), order, preferred_element_type=f32)
    placed = placed[0:64] + placed[64:128]
    for block in range(out_ref.shape[0] // 8):
        tiles = [placed[8 * m : 8 * m + 8, block * 128 : (block + 1) * 128] for m in range(8)]
        tiles = swap_lanes(tiles, 16)
        for slot in range(8):
            out_ref[block * 8 + slot] = tiles[slot]


def inverse_z_body(in_ref, hi_ref, lo_ref, conv_ref, out_ref, rows_ref):
    groups = C // 4
    zero = jnp.zeros((8, 128), jnp.float32)
    for group in range(groups):
        tiles = swap_lanes([in_ref[group * 3 + part] for part in range(3)] + [zero], 16)
        for x in range(4):
            rows_ref[32 * group + 8 * x : 32 * group + 8 * x + 8, :] = tiles[x]
    cells = dot(rows_ref[...], hi_ref[...], lo_ref[...])
    for group in range(groups):
        lanes = slice(group * 256, (group + 1) * 256)
        for x in range(4):
            at = 32 * group + 8 * x
            out_ref[x, :, lanes] = gelu(cells[at : at + 8] + conv_ref[x, :, lanes])


def on_chip(value):
    return pltpu.with_memory_space_constraint(value, pltpu.VMEM)


def local_call(body, out_shape, scratch, *operands, keep=True, remote=(), more=()):
    shapes = [out_shape, *more]
    kinds = [pltpu.VMEM if keep else jax.ShapeDtypeStruct] + [pltpu.VMEM] * len(more)
    inside = pl.BlockSpec(memory_space=pltpu.VMEM)
    outside = pl.BlockSpec(memory_space=pltpu.HBM)
    results = pl.pallas_call(
        body,
        out_shape=[kind(shape, jnp.float32) for kind, shape in zip(kinds, shapes)],
        in_specs=[outside if at in remote else inside for at in range(len(operands))],
        out_specs=[inside] * len(shapes),
        scratch_shapes=scratch,
        compiler_params=pltpu.CompilerParams(vmem_limit_bytes=(62 if remote else 24) << 20),
    )(*operands)
    return results if more else results[0]


def complex_product(spec, table, real, imag):
    cosine = jnp.asarray(table.real.astype(np.float32))
    sine = jnp.asarray(table.imag.astype(np.float32))

    def product(left, right):
        return jnp.einsum(spec, left, right, precision=highest)

    return (
        product(cosine, real) - product(sine, imag),
        product(cosine, imag) + product(sine, real),
    )


def transform(wave_x, wave_y, parts, split_to):
    a, b, y, _, x, _, _ = parts.shape
    shaped = jnp.transpose(parts, (3, 0, 4, 1, 2, 5, 6)).reshape(2, a * x, b * y, 4, 4)
    real, imag = complex_product("qy,xykj->xqkj", wave_y, shaped[0], shaped[1])
    real, imag = complex_product("px,xqkj->pqkj", wave_x, real, imag)
    return jnp.stack([real, imag]).reshape((2,) + split_to + (4, 4))


def on_device(state_field, conv_first, conv_second, spec_real, spec_imag):
    rows_here, cols_here = state_field.shape[:2]
    kept_x, kept_y = spec_real.shape[:2]
    count_x, count_y = lax.axis_size("gx"), lax.axis_size("gy")
    devices = count_x * count_y
    total_x, total_y = rows_here * count_x, cols_here * count_y
    groups, thirds = C // 4, MZ // 4
    owners = groups * thirds
    if (rows_here, cols_here) != (4, 8) or owners > devices:
        raise ValueError("unsupported block")
    both = ("gx", "gy")
    row_start = lax.axis_index("gx") * rows_here
    col_start = lax.axis_index("gy") * cols_here
    f32 = jnp.float32

    wave_z = dft_wave(np.arange(MZ), Z, -1.0).reshape(thirds, 4, Z)
    wave_z = np.concatenate([wave_z, np.zeros((1, 4, Z))])
    parts_z = np.stack([wave_z.real, wave_z.imag])
    forward_z = np.einsum("egrz,ck->czegkr", parts_z, np.eye(4)).reshape(4 * Z, 128)
    gains = np.where(np.arange(16) == 0, 1.0, 2.0).reshape(4, 4) / (total_x * total_y * Z)
    inverse_z = np.einsum("egrz,gr,ck->egcrkz", parts_z, gains, np.eye(4)).reshape(128, 4 * Z)
    forward_x = dft_wave(mode_freqs(MX, total_x), total_x, -1.0)
    forward_y = dft_wave(mode_freqs(MY, total_y), total_y, -1.0)
    inverse_x, inverse_y = np.conj(forward_x).T, np.conj(forward_y).T

    def trade(block):
        return lax.all_to_all(block, both, 0, 0, tiled=True)

    def shift(block, axis, ahead):
        steps = range(lax.axis_size(axis) - 1)
        return lax.ppermute(block, axis, [(i, i + 1) if ahead else (i + 1, i) for i in steps])

    fast = (count_x, count_y, kept_x, kept_y) == (8, 4, 4, 8)

    edge = (2, cols_here, C * Z)
    columns, head, tail = local_call(
        forward_z_body,
        (devices, 8, 128),
        [
            pltpu.VMEM((rows_here, cols_here, C * Z), f32),
            pltpu.VMEM((2, 4 * Z, 128), BF),
            pltpu.SemaphoreType.DMA((2,)),
        ],
        state_field,
        np.stack(halves(forward_z)),
        keep=False,
        remote=(0, 1),
        more=(edge, edge),
    )
    columns = trade(columns)
    top, bottom = shift(tail, "gx", True), shift(head, "gx", False)

    if fast:
        modes = local_call(
            plane_body,
            (devices, 8, 128),
            [pltpu.VMEM((256, 128), f32)],
            on_chip(columns),
            plane_table(line_table(forward_x, count_x, kept_x, count_x, rows_here), forward_y),
            keep=False,
        )
    else:
        parts = columns.reshape(count_x, count_y, cols_here, 2, rows_here, 4, 4)
        modes = transform(forward_x, forward_y, parts, (count_x, kept_x, count_y, kept_y))
        modes = jnp.transpose(modes, (1, 3, 4, 0, 2, 5, 6))
        modes = modes.reshape(devices, kept_y, 2 * kept_x * 16)
    modes = trade(modes)
    parts = (top, state_field, bottom)
    last = jnp.concatenate([part[:, cols_here - 2 :] for part in parts], axis=0)
    first = jnp.concatenate([part[:, :2] for part in parts], axis=0)
    left, right = shift(last, "gy", True), shift(first, "gy", False)
    places = jnp.arange(128, dtype=jnp.int32)[None, :] + 2
    cell_x = row_start - 2 + places // 16
    cell_y = col_start - 2 + places % 16
    inside = (cell_x >= 0) & (cell_x < total_x) & (cell_y >= 0) & (cell_y < total_y)
    mask = inside.astype(f32)

    if fast:
        mixed = local_call(
            mix_body,
            (devices, 8, 128),
            [pltpu.VMEM((32 * groups, 128), f32)]
            + [pltpu.VMEM((4, kept_x, groups, kept_y, MZ * C), f32)] * 2
            + [pltpu.SemaphoreType.DMA((4, 2))],
            on_chip(modes),
            *[
                jnp.transpose(spec, (0, 2, 1, 3)).reshape(kept_x, groups, 4, kept_y, MZ * C)
                for spec in (spec_real, spec_imag)
            ],
            keep=False,
            remote=(1, 2),
        )
    else:
        modes = modes[:owners].reshape(groups, thirds, kept_y, 2, kept_x, 4, 4)
        modes = jnp.transpose(modes, (3, 4, 2, 0, 5, 1, 6))
        modes = modes.reshape(2, kept_x, kept_y, C, MZ)
        weight_real = spec_real.reshape(kept_x, kept_y, C, MZ, C)
        weight_imag = spec_imag.reshape(kept_x, kept_y, C, MZ, C)

        def product(left, right):
            return jnp.einsum("abik,abiko->abok", left, right, precision=highest)

        mixed = jnp.stack(
            [
                product(modes[0], weight_real) - product(modes[1], weight_imag),
                product(modes[0], weight_imag) + product(modes[1], weight_real),
            ]
        ).reshape(2, kept_x, kept_y, groups, 4, thirds, 4)
        mixed = jnp.transpose(mixed, (3, 5, 2, 0, 1, 4, 6))
        mixed = mixed.reshape(owners, kept_y, 2 * kept_x * 16)
        mixed = jnp.pad(mixed, ((0, devices - owners), (0, 0), (0, 0)))
    mixed = trade(mixed)
    filters = [pltpu.VMEM((9 * BLOCK, DEPTH), f32)] + [pltpu.VMEM((9 * BLOCK, DEPTH), BF)] * 2
    hidden = local_call(
        first_conv_body,
        (ROWS + 2 * TOP, 128),
        [
            pltpu.VMEM((8, 16, C * Z), f32),
            pltpu.VMEM((ROWS, 128), f32),
            pltpu.VMEM((ROWS + 2 * TOP, 128), f32),
        ]
        + filters,
        state_field,
        top,
        bottom,
        left,
        right,
        conv_first,
        mask,
    )

    if fast:
        back = local_call(
            plane_body,
            (devices, 8, 128),
            [pltpu.VMEM((256, 128), f32)],
            on_chip(mixed),
            plane_table(line_table(inverse_x, count_x, rows_here, count_x, kept_x), inverse_y),
            keep=False,
        )
    else:
        parts = mixed.reshape(count_x, count_y, kept_y, 2, kept_x, 4, 4)
        back = transform(inverse_x, inverse_y, parts, (count_x, rows_here, count_y, cols_here))
        back = jnp.transpose(back, (1, 3, 4, 0, 2, 5, 6)).reshape(devices, 8, 128)
    back = trade(back)
    conv_out = local_call(
        second_conv_body,
        (rows_here, cols_here, C * Z),
        [pltpu.VMEM((ROWS, 128), f32)] + filters,
        on_chip(hidden),
        conv_second,
    )
    return local_call(
        inverse_z_body,
        (rows_here, cols_here, C * Z),
        [pltpu.VMEM((32 * groups, 128), f32)],
        on_chip(back),
        *halves(inverse_z),
        on_chip(conv_out),
        keep=False,
    )


def solution(mesh):
    in_specs = (P("gx", "gy", None), P(), P(), P("gx", "gy", None, None), P("gx", "gy", None, None))
    out_specs = P("gx", "gy", None)
    return jax.shard_map(on_device, mesh=mesh, in_specs=in_specs, out_specs=out_specs, check_vma=False)
```

```python
import numpy as np
import jax
import jax.numpy as jnp
from jax import lax
from jax.experimental import pallas as pl
from jax.experimental.pallas import tpu as pltpu
from jax.sharding import PartitionSpec as P


C = 36
Z = 64
MX = 16
MY = 16
MZ = 12
BF = jnp.bfloat16
highest = lax.Precision.HIGHEST


def gelu(x):
    return 0.5 * x * (1.0 + lax.erf(x * 0.7071067811865476))


def split(x):
    hi = x.astype(BF)
    return hi, (x - hi.astype(jnp.float32)).astype(BF)


STEP = 4
TOP = 40
DEPTH = 224
ROWS = Z * C
BLOCK = STEP * C


def load_filters(filter_ref, wide_ref, hi_ref, lo_ref):
    wide_ref[...] = jnp.zeros_like(wide_ref)
    for s in range(9):
        taps = filter_ref[s // 3, s % 3]
        for z in range(STEP):
            at = s * BLOCK + z * C
            lane = TOP - C + C * z
            wide_ref[at : at + C, lane : lane + 3 * C] = taps
    hi_ref[...], lo_ref[...] = split(wide_ref[...])


def convolve(data_ref, hi_ref, lo_ref, store):
    f32 = jnp.float32

    def step(g, carry):
        at = pl.multiple_of(g * 2 * BLOCK, 8)
        window = jnp.concatenate(
            [data_ref[pl.ds(pl.multiple_of(at + h * BLOCK, 8), DEPTH), :] for h in range(2)], axis=1
        )
        data_hi, data_lo = split(window)
        total = None
        for s in range(9):
            hi = hi_ref[s * BLOCK : (s + 1) * BLOCK, :]
            lo = lo_ref[s * BLOCK : (s + 1) * BLOCK, :]
            part = jnp.dot(hi, data_hi, preferred_element_type=f32) + (
                jnp.dot(lo, data_hi, preferred_element_type=f32)
                + jnp.dot(hi, data_lo, preferred_element_type=f32)
            )
            halves = [part[:, :128], part[:, 128:]]
            shift = (s // 3 - 1) * 16 + s % 3 - 1
            if shift:
                halves = [pltpu.roll(half, -shift % 128, 1) for half in halves]
            total = halves if total is None else [u + v for u, v in zip(total, halves)]
        for h in range(2):
            store(pl.multiple_of(at + h * BLOCK, 8), total[h])
        return carry

    lax.fori_loop(0, Z // (2 * STEP), step, 0)


def odd_row():
    return (lax.axis_index("gx") & 1) == 1


def first_conv_body(
    cells_ref, near_ref, far_ref, left_ref, right_ref, filter_ref, mask_ref,
    out_ref, frame_ref, turn_ref, data_ref, wide_ref, hi_ref, lo_ref,
):
    f32 = jnp.float32
    frame_ref[:, 8:16, :] = jnp.zeros((8, 8, C * Z), f32)
    frame_ref[2:6, 0:8, :] = cells_ref[...]

    @pl.when(odd_row())
    def _():
        frame_ref[0:2, 0:8, :] = near_ref[...]
        frame_ref[6:8, 0:8, :] = far_ref[...]

    @pl.when(jnp.logical_not(odd_row()))
    def _():
        frame_ref[0:2, 0:8, :] = far_ref[...]
        frame_ref[6:8, 0:8, :] = near_ref[...]

    for x in range(8):
        frame_ref[x, 8:10, :] = right_ref[x]
        frame_ref[(x + 7) % 8, 14:16, :] = left_ref[x]
    data_ref[0:TOP, :] = jnp.zeros((TOP, 128), f32)
    data_ref[TOP + ROWS :, :] = jnp.zeros((TOP, 128), f32)
    for j in range(C * Z // 128):
        lanes = slice(j * 128, (j + 1) * 128)
        turn_ref[lanes, :] = frame_ref[:, :, lanes].reshape(128, 128).T
    for z in range(Z):
        data_ref[TOP + z * C : TOP + (z + 1) * C, :] = turn_ref[pl.ds(z, C, stride=Z), :]
    load_filters(filter_ref, wide_ref, hi_ref, lo_ref)
    mask = mask_ref[0:1, :]

    def store(at, total):
        turn_ref[pl.ds(at, BLOCK), :] = gelu(total) * mask

    convolve(data_ref, hi_ref, lo_ref, store)
    out_ref[0:TOP, :] = jnp.zeros((TOP, 128), f32)
    out_ref[TOP + ROWS :, :] = jnp.zeros((TOP, 128), f32)
    out_ref[TOP : TOP + ROWS, :] = turn_ref[...]


def second_conv_body(data_ref, filter_ref, out_ref, turn_ref, wide_ref, hi_ref, lo_ref):
    load_filters(filter_ref, wide_ref, hi_ref, lo_ref)

    def store(at, total):
        turn_ref[pl.ds(at, BLOCK), :] = total

    convolve(data_ref, hi_ref, lo_ref, store)
    for j in range(C * Z // 128):
        pieces = [turn_ref[pl.ds(2 * j + e, Z, stride=C), :] for e in range(2)]
        turned = jnp.concatenate(pieces, axis=0).T
        for x in range(4):
            out_ref[x, :, j * 128 : (j + 1) * 128] = turned[16 * x + 32 : 16 * x + 40, :]


def dft_wave(freqs, length, sign):
    angle = sign * 2.0 * np.pi * np.outer(freqs, np.arange(length)) / length
    return np.cos(angle) + 1j * np.sin(angle)


def mode_freqs(kept, length):
    places = np.arange(2 * kept)
    return np.where(places < kept, places, places + length - 2 * kept)


def halves(table):
    hi = table.astype(BF)
    lo = (table - hi.astype(np.float64)).astype(BF)
    return hi, lo


def line_table(wave, outer_to, inner_to, outer, inner):
    shaped = wave.reshape(outer_to, inner_to, outer, inner)
    turned = np.stack([shaped, shaped * 1j])
    parts = np.stack([turned.real, turned.imag])
    table = np.einsum("crAmal,uv->rlaucmAv", parts, np.eye(2))
    return table.reshape(4 * inner * outer, 4 * inner_to * outer_to)


def plane_table(lines, wave):
    cross = np.concatenate([wave.real, wave.imag])
    cross = np.pad(cross, ((0, 0), (0, lines.shape[1] - cross.shape[1])))
    return np.stack(halves(np.concatenate([lines, cross])))


def dot(left, right_hi, right_lo):
    f32 = jnp.float32
    hi, lo = split(left)
    return jnp.dot(hi, right_hi, preferred_element_type=f32) + (
        jnp.dot(lo, right_hi, preferred_element_type=f32)
        + jnp.dot(hi, right_lo, preferred_element_type=f32)
    )


def swap_lanes(tiles, low):
    tiles = list(tiles)
    lane = lax.broadcasted_iota(jnp.int32, (8, 128), 1)
    bit = 1
    while bit < len(tiles):
        width = low * bit
        upper = (lane & width) != 0
        for at in range(len(tiles)):
            if at & bit == 0:
                first, second = tiles[at], tiles[at | bit]
                tiles[at] = jnp.where(upper, pltpu.roll(second, width, 1), first)
                tiles[at | bit] = jnp.where(upper, second, pltpu.roll(first, 128 - width, 1))
        bit *= 2
    return tiles


def forward_z_body(
    field_ref, waves_ref, out_ref, near_ref, far_ref, first_ref, last_ref, cells_ref, table_ref, sems
):
    groups = C // 4
    copies = [
        pltpu.make_async_copy(field_ref, cells_ref, sems.at[0]),
        pltpu.make_async_copy(waves_ref, table_ref, sems.at[1]),
    ]
    for copy in copies:
        copy.start()
    for copy in copies:
        copy.wait()
    rows = cells_ref.shape[0]
    cols = cells_ref.shape[1]
    first_ref[...] = cells_ref[:, 0:2, :]
    last_ref[...] = cells_ref[:, cols - 2 : cols, :]

    @pl.when(odd_row())
    def _():
        near_ref[...] = cells_ref[0:2]
        far_ref[...] = cells_ref[rows - 2 : rows]

    @pl.when(jnp.logical_not(odd_row()))
    def _():
        near_ref[...] = cells_ref[rows - 2 : rows]
        far_ref[...] = cells_ref[0:2]

    stacked = jnp.concatenate(
        [cells_ref[:, :, g * 256 : (g + 1) * 256].reshape(32, 256) for g in range(groups)], axis=0
    )
    waves = dot(stacked, table_ref[0], table_ref[1])
    for group in range(groups):
        at = 32 * group
        tiles = swap_lanes([waves[at + 8 * x : at + 8 * x + 8] for x in range(4)], 16)
        for part in range(3):
            out_ref[group * 3 + part] = tiles[part]
    for spare in range(3 * groups, out_ref.shape[0]):
        out_ref[spare] = jnp.zeros((8, 128), jnp.float32)


def plane_body(in_ref, table_ref, out_ref, rows_ref):
    f32 = jnp.float32
    outer, inner = 8, 4
    for b in range(inner):
        tiles = swap_lanes([in_ref[a * inner + b] for a in range(outer)], 2)
        for g in range(8):
            rows_ref[g * 32 + b * 8 : g * 32 + b * 8 + 8, :] = tiles[g]
    lines = dot(rows_ref[...], table_ref[0, 0:128, :], table_ref[1, 0:128, :])
    minus = lax.broadcasted_iota(jnp.int32, (32, 128), 1) < 64
    results = []
    cross_hi, cross_lo = table_ref[0, 128:192, 0:32], table_ref[1, 128:192, 0:32]
    for g in range(0, 8, 2):
        part = jnp.concatenate([lines[g * 32 : g * 32 + 32], lines[g * 32 + 32 : g * 32 + 64]], axis=1)
        hi, lo = split(part)
        both = jnp.dot(cross_hi, hi, preferred_element_type=f32) + (
            jnp.dot(cross_lo, hi, preferred_element_type=f32)
            + jnp.dot(cross_hi, lo, preferred_element_type=f32)
        )
        for h in range(2):
            turned = pltpu.roll(both[32:, h * 128 : h * 128 + 128], 64, 1)
            plain = both[:32, h * 128 : h * 128 + 128]
            results.append(jnp.where(minus, plain - turned, plain + turned))
    for b in range(inner):
        tiles = swap_lanes([results[g][b * 8 : b * 8 + 8] for g in range(8)], 2)
        for a in range(outer):
            out_ref[a * inner + b] = tiles[a]


def mode_of(place):
    return jnp.floor((place.astype(jnp.float32) + 0.5) * (1.0 / C)).astype(jnp.int32)


def mix_body(in_ref, real_hbm, imag_hbm, out_ref, left_ref, real_ref, imag_ref, sems):
    f32 = jnp.float32
    groups = C // 4
    copies = [
        [
            pltpu.make_async_copy(source.at[:, :, k], held.at[k], sems.at[k, e])
            for e, (source, held) in enumerate(((real_hbm, real_ref), (imag_hbm, imag_ref)))
        ]
        for k in range(4)
    ]
    for pair in copies:
        for copy in pair:
            copy.start()
    width = MZ * C
    lane = lax.broadcasted_iota(jnp.int32, (256, width), 0) & 127
    mode = mode_of(lax.broadcasted_iota(jnp.int32, (1, width), 1))
    wanted = lane - ((mode >> 2) * 16 + (mode & 3))
    place = lax.broadcasted_iota(jnp.int32, (width, 1), 0)
    mode = mode_of(place)
    channel = place - mode * C
    column = ((channel >> 2) * 3 + (mode >> 2)) * 16 + (channel & 3) * 4 + (mode & 3)
    slots = lax.broadcasted_iota(jnp.int32, (width, out_ref.shape[0] * 16), 1)
    order = jnp.where(slots == column, 1.0, 0.0).astype(BF)
    zero = jnp.zeros((8, 128), f32)
    for group in range(groups):
        tiles = swap_lanes([in_ref[group * 3 + part] for part in range(3)] + [zero], 16)
        for m in range(4):
            at = (m * groups + group) * 8
            left_ref[at : at + 8, :] = tiles[m]
    hi, lo = split(left_ref[...])
    left = jnp.concatenate([hi, lo], axis=1)
    real = [jnp.zeros((8, MZ * C), f32) for _ in range(4)]
    imag = [jnp.zeros((8, MZ * C), f32) for _ in range(4)]
    for k in range(4):
        sides = []
        for e in range(2):
            table = jnp.where(wanted == e * 64 + k * 4, 1.0, 0.0).astype(BF)
            sides.append(jnp.dot(left, table, preferred_element_type=f32))
        for copy in copies[k]:
            copy.wait()
        for m in range(4):
            for group in range(groups):
                at = (m * groups + group) * 8
                re = sides[0][at : at + 8]
                im = sides[1][at : at + 8]
                wr = real_ref[k, m, group]
                wi = imag_ref[k, m, group]
                real[m] = real[m] + (re * wr - im * wi)
                imag[m] = imag[m] + (re * wi + im * wr)
    hi, lo = split(jnp.concatenate(real + imag, axis=0))
    placed = jnp.dot(jnp.concatenate([hi, lo], axis=0), order, preferred_element_type=f32)
    placed = placed[0:64] + placed[64:128]
    for block in range(out_ref.shape[0] // 8):
        tiles = [placed[8 * m : 8 * m + 8, block * 128 : (block + 1) * 128] for m in range(8)]
        tiles = swap_lanes(tiles, 16)
        for slot in range(8):
            out_ref[block * 8 + slot] = tiles[slot]


def inverse_z_body(in_ref, hi_ref, lo_ref, conv_ref, out_ref, rows_ref):
    groups = C // 4
    zero = jnp.zeros((8, 128), jnp.float32)
    for group in range(groups):
        tiles = swap_lanes([in_ref[group * 3 + part] for part in range(3)] + [zero], 16)
        for x in range(4):
            rows_ref[32 * group + 8 * x : 32 * group + 8 * x + 8, :] = tiles[x]
    cells = dot(rows_ref[...], hi_ref[...], lo_ref[...])
    for group in range(groups):
        lanes = slice(group * 256, (group + 1) * 256)
        for x in range(4):
            at = 32 * group + 8 * x
            out_ref[x, :, lanes] = gelu(cells[at : at + 8] + conv_ref[x, :, lanes])


def on_chip(value):
    return pltpu.with_memory_space_constraint(value, pltpu.VMEM)


def local_call(body, out_shape, scratch, *operands, keep=True, remote=(), more=()):
    shapes = [out_shape, *more]
    kinds = [pltpu.VMEM if keep else jax.ShapeDtypeStruct] + [pltpu.VMEM] * len(more)
    inside = pl.BlockSpec(memory_space=pltpu.VMEM)
    outside = pl.BlockSpec(memory_space=pltpu.HBM)
    results = pl.pallas_call(
        body,
        out_shape=[kind(shape, jnp.float32) for kind, shape in zip(kinds, shapes)],
        in_specs=[outside if at in remote else inside for at in range(len(operands))],
        out_specs=[inside] * len(shapes),
        scratch_shapes=scratch,
        compiler_params=pltpu.CompilerParams(vmem_limit_bytes=(62 if remote else 24) << 20),
    )(*operands)
    return results if more else results[0]


def complex_product(spec, table, real, imag):
    cosine = jnp.asarray(table.real.astype(np.float32))
    sine = jnp.asarray(table.imag.astype(np.float32))

    def product(left, right):
        return jnp.einsum(spec, left, right, precision=highest)

    return (
        product(cosine, real) - product(sine, imag),
        product(cosine, imag) + product(sine, real),
    )


def transform(wave_x, wave_y, parts, split_to):
    a, b, y, _, x, _, _ = parts.shape
    shaped = jnp.transpose(parts, (3, 0, 4, 1, 2, 5, 6)).reshape(2, a * x, b * y, 4, 4)
    real, imag = complex_product("qy,xykj->xqkj", wave_y, shaped[0], shaped[1])
    real, imag = complex_product("px,xqkj->pqkj", wave_x, real, imag)
    return jnp.stack([real, imag]).reshape((2,) + split_to + (4, 4))


def on_device(state_field, conv_first, conv_second, spec_real, spec_imag):
    rows_here, cols_here = state_field.shape[:2]
    kept_x, kept_y = spec_real.shape[:2]
    count_x, count_y = lax.axis_size("gx"), lax.axis_size("gy")
    devices = count_x * count_y
    total_x, total_y = rows_here * count_x, cols_here * count_y
    groups, thirds = C // 4, MZ // 4
    owners = groups * thirds
    if (rows_here, cols_here) != (4, 8) or owners > devices:
        raise ValueError("unsupported block")
    both = ("gx", "gy")
    row_start = lax.axis_index("gx") * rows_here
    col_start = lax.axis_index("gy") * cols_here
    f32 = jnp.float32

    wave_z = dft_wave(np.arange(MZ), Z, -1.0).reshape(thirds, 4, Z)
    wave_z = np.concatenate([wave_z, np.zeros((1, 4, Z))])
    parts_z = np.stack([wave_z.real, wave_z.imag])
    forward_z = np.einsum("egrz,ck->czegkr", parts_z, np.eye(4)).reshape(4 * Z, 128)
    gains = np.where(np.arange(16) == 0, 1.0, 2.0).reshape(4, 4) / (total_x * total_y * Z)
    inverse_z = np.einsum("egrz,gr,ck->egcrkz", parts_z, gains, np.eye(4)).reshape(128, 4 * Z)
    forward_x = dft_wave(mode_freqs(MX, total_x), total_x, -1.0)
    forward_y = dft_wave(mode_freqs(MY, total_y), total_y, -1.0)
    inverse_x, inverse_y = np.conj(forward_x).T, np.conj(forward_y).T

    def trade(block):
        return lax.all_to_all(block, both, 0, 0, tiled=True)

    def shift(block, axis, ahead):
        steps = range(lax.axis_size(axis) - 1)
        return lax.ppermute(block, axis, [(i, i + 1) if ahead else (i + 1, i) for i in steps])

    fast = (count_x, count_y, kept_x, kept_y) == (8, 4, 4, 8)

    edge, side = (2, cols_here, C * Z), (rows_here, 2, C * Z)
    columns, near, far, first, last = local_call(
        forward_z_body,
        (devices, 8, 128),
        [
            pltpu.VMEM((rows_here, cols_here, C * Z), f32),
            pltpu.VMEM((2, 4 * Z, 128), BF),
            pltpu.SemaphoreType.DMA((2,)),
        ],
        state_field,
        np.stack(halves(forward_z)),
        keep=False,
        remote=(0, 1),
        more=(edge, edge, side, side),
    )
    columns = trade(columns)
    ends = range(1, count_x - 1)
    near = lax.ppermute(near, "gx", [(i, i ^ 1) for i in range(count_x) if i ^ 1 < count_x])
    far = lax.ppermute(far, "gx", [(i, (i + 1 ^ 1) - 1) for i in ends])

    if fast:
        modes = local_call(
            plane_body,
            (devices, 8, 128),
            [pltpu.VMEM((256, 128), f32)],
            on_chip(columns),
            plane_table(line_table(forward_x, count_x, kept_x, count_x, rows_here), forward_y),
            keep=False,
        )
    else:
        parts = columns.reshape(count_x, count_y, cols_here, 2, rows_here, 4, 4)
        modes = transform(forward_x, forward_y, parts, (count_x, kept_x, count_y, kept_y))
        modes = jnp.transpose(modes, (1, 3, 4, 0, 2, 5, 6))
        modes = modes.reshape(devices, kept_y, 2 * kept_x * 16)
    modes = trade(modes)
    odd = lax.axis_index("gx") % 2 == 1

    def framed(middle, low):
        pair = near[:, low : low + 2], far[:, low : low + 2]
        top, bottom = jnp.where(odd, pair[0], pair[1]), jnp.where(odd, pair[1], pair[0])
        return jnp.concatenate([top, middle, bottom], axis=0)

    last, first = framed(last, cols_here - 2), framed(first, 0)
    left, right = shift(last, "gy", True), shift(first, "gy", False)
    places = jnp.arange(128, dtype=jnp.int32)[None, :] + 2
    cell_x = row_start - 2 + places // 16
    cell_y = col_start - 2 + places % 16
    inside = (cell_x >= 0) & (cell_x < total_x) & (cell_y >= 0) & (cell_y < total_y)
    mask = inside.astype(f32)

    if fast:
        mixed = local_call(
            mix_body,
            (devices, 8, 128),
            [pltpu.VMEM((32 * groups, 128), f32)]
            + [pltpu.VMEM((4, kept_x, groups, kept_y, MZ * C), f32)] * 2
            + [pltpu.SemaphoreType.DMA((4, 2))],
            on_chip(modes),
            *[
                jnp.transpose(spec, (0, 2, 1, 3)).reshape(kept_x, groups, 4, kept_y, MZ * C)
                for spec in (spec_real, spec_imag)
            ],
            keep=False,
            remote=(1, 2),
        )
    else:
        modes = modes[:owners].reshape(groups, thirds, kept_y, 2, kept_x, 4, 4)
        modes = jnp.transpose(modes, (3, 4, 2, 0, 5, 1, 6))
        modes = modes.reshape(2, kept_x, kept_y, C, MZ)
        weight_real = spec_real.reshape(kept_x, kept_y, C, MZ, C)
        weight_imag = spec_imag.reshape(kept_x, kept_y, C, MZ, C)

        def product(left, right):
            return jnp.einsum("abik,abiko->abok", left, right, precision=highest)

        mixed = jnp.stack(
            [
                product(modes[0], weight_real) - product(modes[1], weight_imag),
                product(modes[0], weight_imag) + product(modes[1], weight_real),
            ]
        ).reshape(2, kept_x, kept_y, groups, 4, thirds, 4)
        mixed = jnp.transpose(mixed, (3, 5, 2, 0, 1, 4, 6))
        mixed = mixed.reshape(owners, kept_y, 2 * kept_x * 16)
        mixed = jnp.pad(mixed, ((0, devices - owners), (0, 0), (0, 0)))
    mixed = trade(mixed)
    filters = [pltpu.VMEM((9 * BLOCK, DEPTH), f32)] + [pltpu.VMEM((9 * BLOCK, DEPTH), BF)] * 2
    hidden = local_call(
        first_conv_body,
        (ROWS + 2 * TOP, 128),
        [
            pltpu.VMEM((8, 16, C * Z), f32),
            pltpu.VMEM((ROWS, 128), f32),
            pltpu.VMEM((ROWS + 2 * TOP, 128), f32),
        ]
        + filters,
        state_field,
        near,
        far,
        left,
        right,
        conv_first,
        mask,
    )

    if fast:
        back = local_call(
            plane_body,
            (devices, 8, 128),
            [pltpu.VMEM((256, 128), f32)],
            on_chip(mixed),
            plane_table(line_table(inverse_x, count_x, rows_here, count_x, kept_x), inverse_y),
            keep=False,
        )
    else:
        parts = mixed.reshape(count_x, count_y, kept_y, 2, kept_x, 4, 4)
        back = transform(inverse_x, inverse_y, parts, (count_x, rows_here, count_y, cols_here))
        back = jnp.transpose(back, (1, 3, 4, 0, 2, 5, 6)).reshape(devices, 8, 128)
    back = trade(back)
    conv_out = local_call(
        second_conv_body,
        (rows_here, cols_here, C * Z),
        [pltpu.VMEM((ROWS, 128), f32)] + filters,
        on_chip(hidden),
        conv_second,
    )
    return local_call(
        inverse_z_body,
        (rows_here, cols_here, C * Z),
        [pltpu.VMEM((32 * groups, 128), f32)],
        on_chip(back),
        *halves(inverse_z),
        on_chip(conv_out),
        keep=False,
    )


def solution(mesh):
    in_specs = (P("gx", "gy", None), P(), P(), P("gx", "gy", None, None), P("gx", "gy", None, None))
    out_specs = P("gx", "gy", None)
    return jax.shard_map(on_device, mesh=mesh, in_specs=in_specs, out_specs=out_specs, check_vma=False)
```

```python
import numpy as np
import jax
import jax.numpy as jnp
from jax import lax
from jax.experimental import pallas as pl
from jax.experimental.pallas import tpu as pltpu
from jax.sharding import PartitionSpec as P


C = 36
Z = 64
MX = 16
MY = 16
MZ = 12
BF = jnp.bfloat16
highest = lax.Precision.HIGHEST


def gelu(x):
    return 0.5 * x * (1.0 + lax.erf(x * 0.7071067811865476))


def split(x):
    hi = x.astype(BF)
    return hi, (x - hi.astype(jnp.float32)).astype(BF)


STEP = 4
TOP = 40
DEPTH = 224
ROWS = Z * C
BLOCK = STEP * C
LATE = 1
EARLY = ROWS - LATE * 2 * BLOCK


def load_filters(filter_ref, wide_ref, hi_ref, lo_ref):
    wide_ref[...] = jnp.zeros_like(wide_ref)
    for s in range(9):
        taps = filter_ref[s // 3, s % 3]
        for z in range(STEP):
            at = s * BLOCK + z * C
            lane = TOP - C + C * z
            wide_ref[at : at + C, lane : lane + 3 * C] = taps
    hi_ref[...], lo_ref[...] = split(wide_ref[...])


def convolve(data_ref, hi_ref, lo_ref, store, pairs):
    f32 = jnp.float32

    def step(g, carry):
        at = pl.multiple_of(g * 2 * BLOCK, 8)
        window = jnp.concatenate(
            [data_ref[pl.ds(pl.multiple_of(at + h * BLOCK, 8), DEPTH), :] for h in range(2)], axis=1
        )
        data_hi, data_lo = split(window)
        total = None
        for s in range(9):
            hi = hi_ref[s * BLOCK : (s + 1) * BLOCK, :]
            lo = lo_ref[s * BLOCK : (s + 1) * BLOCK, :]
            part = jnp.dot(hi, data_hi, preferred_element_type=f32) + (
                jnp.dot(lo, data_hi, preferred_element_type=f32)
                + jnp.dot(hi, data_lo, preferred_element_type=f32)
            )
            halves = [part[:, :128], part[:, 128:]]
            shift = (s // 3 - 1) * 16 + s % 3 - 1
            if shift:
                halves = [pltpu.roll(half, -shift % 128, 1) for half in halves]
            total = halves if total is None else [u + v for u, v in zip(total, halves)]
        for h in range(2):
            store(pl.multiple_of(at + h * BLOCK, 8), total[h])
        return carry

    lax.fori_loop(0, pairs, step, 0)


def odd_row():
    return (lax.axis_index("gx") & 1) == 1


def first_conv_body(
    cells_ref, near_ref, far_ref, left_ref, right_ref, filter_ref, mask_ref,
    out_ref, tail_ref, frame_ref, turn_ref, data_ref, wide_ref, hi_ref, lo_ref,
):
    f32 = jnp.float32
    frame_ref[:, 8:16, :] = jnp.zeros((8, 8, C * Z), f32)
    frame_ref[2:6, 0:8, :] = cells_ref[...]

    @pl.when(odd_row())
    def _():
        frame_ref[0:2, 0:8, :] = near_ref[...]
        frame_ref[6:8, 0:8, :] = far_ref[...]

    @pl.when(jnp.logical_not(odd_row()))
    def _():
        frame_ref[0:2, 0:8, :] = far_ref[...]
        frame_ref[6:8, 0:8, :] = near_ref[...]

    for x in range(8):
        frame_ref[x, 8:10, :] = right_ref[x]
        frame_ref[(x + 7) % 8, 14:16, :] = left_ref[x]
    data_ref[0:TOP, :] = jnp.zeros((TOP, 128), f32)
    data_ref[TOP + ROWS :, :] = jnp.zeros((TOP, 128), f32)
    for j in range(C * Z // 128):
        lanes = slice(j * 128, (j + 1) * 128)
        turn_ref[lanes, :] = frame_ref[:, :, lanes].reshape(128, 128).T
    for z in range(Z):
        data_ref[TOP + z * C : TOP + (z + 1) * C, :] = turn_ref[pl.ds(z, C, stride=Z), :]
    load_filters(filter_ref, wide_ref, hi_ref, lo_ref)
    mask = mask_ref[0:1, :]

    def store(at, total):
        turn_ref[pl.ds(at, BLOCK), :] = gelu(total) * mask

    tail_ref[...] = data_ref[EARLY:, :]
    convolve(data_ref, hi_ref, lo_ref, store, EARLY // (2 * BLOCK))
    out_ref[0:TOP, :] = jnp.zeros((TOP, 128), f32)
    out_ref[TOP:, :] = turn_ref[0:EARLY, :]


HALF = ROWS // 2
PACKED = HALF + 2 * TOP


def second_conv_body(
    data_ref, tail_ref, mask_ref, first_ref, filter_ref, out_ref,
    pack_hi_ref, pack_lo_ref, turn_ref, merge_ref, late_ref, wide_ref, hi_ref, lo_ref,
):
    f32 = jnp.float32
    mask = mask_ref[0:1, :]

    def store(at, total):
        late_ref[pl.ds(at, BLOCK), :] = gelu(total) * mask

    load_filters(first_ref, wide_ref, hi_ref, lo_ref)
    convolve(tail_ref, hi_ref, lo_ref, store, LATE)
    load_filters(filter_ref, wide_ref, hi_ref, lo_ref)
    source = lax.broadcasted_iota(jnp.int32, (256, 128), 0)
    target = lax.broadcasted_iota(jnp.int32, (1, 128), 1)
    place = target & 63
    line = jnp.floor((place.astype(f32) + 0.5) * 0.1).astype(jnp.int32)
    wanted = (target >= 64).astype(jnp.int32) * 128 + 16 * (line + 1) + place - 10 * line - 1
    wanted = jnp.where(place < 60, wanted, -1)
    select = jnp.where(source == wanted, 1.0, 0.0).astype(BF)
    upper = [data_ref[HALF : TOP + EARLY, :], late_ref[...], jnp.zeros((TOP, 128), f32)]
    whole = jnp.concatenate([data_ref[0:PACKED, :], jnp.concatenate(upper, axis=0)], axis=1)
    for part, held_ref in zip(split(whole), (pack_hi_ref, pack_lo_ref)):
        held_ref[...] = jnp.dot(part, select, preferred_element_type=f32).astype(BF)

    def step(g, carry):
        at = pl.multiple_of(g * BLOCK, 16)
        later = pl.multiple_of(at + HALF // 2, 16)
        data_hi, data_lo = [
            jnp.concatenate([held[pl.ds(at, DEPTH), :], held[pl.ds(later, DEPTH), :]], axis=1)
            for held in (pack_hi_ref, pack_lo_ref)
        ]
        total = None
        for s in range(9):
            hi = hi_ref[s * BLOCK : (s + 1) * BLOCK, :]
            lo = lo_ref[s * BLOCK : (s + 1) * BLOCK, :]
            part = jnp.dot(hi, data_hi, preferred_element_type=f32) + (
                jnp.dot(lo, data_hi, preferred_element_type=f32)
                + jnp.dot(hi, data_lo, preferred_element_type=f32)
            )
            sides = [part[:, :128], part[:, 128:]]
            shift = (s // 3 - 1) * 10 + s % 3 - 1
            if shift:
                sides = [pltpu.roll(side, -shift % 128, 1) for side in sides]
            total = sides if total is None else [u + v for u, v in zip(total, sides)]
        turn_ref[pl.ds(at, BLOCK), :] = total[0]
        turn_ref[pl.ds(later, BLOCK), :] = total[1]
        return carry

    lax.fori_loop(0, Z // (4 * STEP), step, 0)
    quarter = lax.broadcasted_iota(jnp.int32, (64, 128), 1) >> 5
    for four in range(C // 4):
        pieces = [turn_ref[pl.ds(4 * four + e, Z // 2, stride=C), :] for e in range(4)]
        turned = jnp.concatenate(pieces, axis=0).T
        early, late = turned[:64], turned[64:]
        for pair in range(2):
            turns = ((0, 32, 32, 64), (64, 96, 96, 0))[pair]
            parts = [
                pltpu.roll(side, turn, 1) if turn else side
                for side, turn in zip((early, late, early, late), turns)
            ]
            merge_ref[pair] = jnp.where(
                quarter < 2,
                jnp.where(quarter < 1, parts[0], parts[1]),
                jnp.where(quarter < 3, parts[2], parts[3]),
            )
            at = (2 * four + pair) * 128
            for x in range(4):
                out_ref[x, :, at : at + 128] = merge_ref[pair, 10 * x + 11 : 10 * x + 19, :]


def dft_wave(freqs, length, sign):
    angle = sign * 2.0 * np.pi * np.outer(freqs, np.arange(length)) / length
    return np.cos(angle) + 1j * np.sin(angle)


def mode_freqs(kept, length):
    places = np.arange(2 * kept)
    return np.where(places < kept, places, places + length - 2 * kept)


def halves(table):
    hi = table.astype(BF)
    lo = (table - hi.astype(np.float64)).astype(BF)
    return hi, lo


def line_table(wave, outer_to, inner_to, outer, inner):
    shaped = wave.reshape(outer_to, inner_to, outer, inner)
    turned = np.stack([shaped, shaped * 1j])
    parts = np.stack([turned.real, turned.imag])
    table = np.einsum("crAmal,uv->rlaucmAv", parts, np.eye(2))
    return table.reshape(4 * inner * outer, 4 * inner_to * outer_to)


def plane_table(lines, wave):
    cross = np.concatenate([wave.real, wave.imag])
    cross = np.pad(cross, ((0, 0), (0, lines.shape[1] - cross.shape[1])))
    return np.stack(halves(np.concatenate([lines, cross])))


def dot(left, right_hi, right_lo):
    f32 = jnp.float32
    hi, lo = split(left)
    return jnp.dot(hi, right_hi, preferred_element_type=f32) + (
        jnp.dot(lo, right_hi, preferred_element_type=f32)
        + jnp.dot(hi, right_lo, preferred_element_type=f32)
    )


def swap_lanes(tiles, low):
    tiles = list(tiles)
    lane = lax.broadcasted_iota(jnp.int32, (8, 128), 1)
    bit = 1
    while bit < len(tiles):
        width = low * bit
        upper = (lane & width) != 0
        for at in range(len(tiles)):
            if at & bit == 0:
                first, second = tiles[at], tiles[at | bit]
                tiles[at] = jnp.where(upper, pltpu.roll(second, width, 1), first)
                tiles[at | bit] = jnp.where(upper, second, pltpu.roll(first, 128 - width, 1))
        bit *= 2
    return tiles


def forward_z_body(
    field_ref, waves_ref, lines_ref, out_ref, near_ref, far_ref, first_ref, last_ref, held_ref,
    cells_ref, table_ref, sems,
):
    groups = C // 4
    copies = [
        pltpu.make_async_copy(field_ref, cells_ref, sems.at[0]),
        pltpu.make_async_copy(waves_ref, table_ref, sems.at[1]),
    ]
    later = pltpu.make_async_copy(lines_ref, held_ref, sems.at[2])
    for copy in copies:
        copy.start()
    later.start()
    for copy in copies:
        copy.wait()
    rows = cells_ref.shape[0]
    cols = cells_ref.shape[1]
    first_ref[...] = cells_ref[:, 0:2, :]
    last_ref[...] = cells_ref[:, cols - 2 : cols, :]

    @pl.when(odd_row())
    def _():
        near_ref[...] = cells_ref[0:2]
        far_ref[...] = cells_ref[rows - 2 : rows]

    @pl.when(jnp.logical_not(odd_row()))
    def _():
        near_ref[...] = cells_ref[rows - 2 : rows]
        far_ref[...] = cells_ref[0:2]

    stacked = jnp.concatenate(
        [cells_ref[:, :, g * 256 : (g + 1) * 256].reshape(32, 256) for g in range(groups)], axis=0
    )
    waves = dot(stacked, table_ref[0], table_ref[1])
    for group in range(groups):
        at = 32 * group
        tiles = swap_lanes([waves[at + 8 * x : at + 8 * x + 8] for x in range(4)], 16)
        for part in range(3):
            out_ref[group * 3 + part] = tiles[part]
    for spare in range(3 * groups, out_ref.shape[0]):
        out_ref[spare] = jnp.zeros((8, 128), jnp.float32)
    later.wait()


def plane_body(in_ref, table_ref, out_ref, rows_ref):
    f32 = jnp.float32
    outer, inner = 8, 4
    for b in range(inner):
        tiles = swap_lanes([in_ref[a * inner + b] for a in range(outer)], 2)
        for g in range(8):
            rows_ref[g * 32 + b * 8 : g * 32 + b * 8 + 8, :] = tiles[g]
    lines = dot(rows_ref[...], table_ref[0, 0:128, :], table_ref[1, 0:128, :])
    minus = lax.broadcasted_iota(jnp.int32, (32, 128), 1) < 64
    results = []
    cross_hi, cross_lo = table_ref[0, 128:192, 0:32], table_ref[1, 128:192, 0:32]
    for g in range(0, 8, 2):
        part = jnp.concatenate([lines[g * 32 : g * 32 + 32], lines[g * 32 + 32 : g * 32 + 64]], axis=1)
        hi, lo = split(part)
        both = jnp.dot(cross_hi, hi, preferred_element_type=f32) + (
            jnp.dot(cross_lo, hi, preferred_element_type=f32)
            + jnp.dot(cross_hi, lo, preferred_element_type=f32)
        )
        for h in range(2):
            turned = pltpu.roll(both[32:, h * 128 : h * 128 + 128], 64, 1)
            plain = both[:32, h * 128 : h * 128 + 128]
            results.append(jnp.where(minus, plain - turned, plain + turned))
    for b in range(inner):
        tiles = swap_lanes([results[g][b * 8 : b * 8 + 8] for g in range(8)], 2)
        for a in range(outer):
            out_ref[a * inner + b] = tiles[a]


def mode_of(place):
    return jnp.floor((place.astype(jnp.float32) + 0.5) * (1.0 / C)).astype(jnp.int32)


def mix_body(in_ref, real_hbm, imag_hbm, out_ref, left_ref, real_ref, imag_ref, sides_ref, sems):
    f32 = jnp.float32
    groups = C // 4
    copies = [
        [
            pltpu.make_async_copy(source.at[k], held.at[k], sems.at[k, e])
            for e, (source, held) in enumerate(((real_hbm, real_ref), (imag_hbm, imag_ref)))
        ]
        for k in range(4)
    ]
    for pair in copies:
        for copy in pair:
            copy.start()
    width = MZ * C
    lane = lax.broadcasted_iota(jnp.int32, (128, width), 0)
    mode = mode_of(lax.broadcasted_iota(jnp.int32, (1, width), 1))
    table = jnp.where(lane == (mode >> 2) * 16 + (mode & 3), 1.0, 0.0).astype(BF)
    table = jnp.concatenate([table, table], axis=0)
    place = lax.broadcasted_iota(jnp.int32, (width, 1), 0)
    mode = mode_of(place)
    channel = place - mode * C
    column = ((channel >> 2) * 3 + (mode >> 2)) * 16 + (channel & 3) * 4 + (mode & 3)
    slots = lax.broadcasted_iota(jnp.int32, (width, out_ref.shape[0] * 16), 1)
    order = jnp.where(slots == column, 1.0, 0.0).astype(BF)
    zero = jnp.zeros((8, 128), f32)
    for group in range(groups):
        tiles = swap_lanes([in_ref[group * 3 + part] for part in range(3)] + [zero], 16)
        for m in range(4):
            at = (m * groups + group) * 8
            left_ref[at : at + 8, :] = tiles[m]
    left = left_ref[...]
    real = [jnp.zeros((8, MZ * C), f32) for _ in range(4)]
    imag = [jnp.zeros((8, MZ * C), f32) for _ in range(4)]
    for k in range(4):
        for e in range(2):
            turn = -(e * 64 + k * 4) % 128
            hi, lo = split(pltpu.roll(left, turn, 1) if turn else left)
            turned = jnp.concatenate([hi, lo], axis=1)
            sides_ref[2 * k + e] = jnp.dot(turned, table, preferred_element_type=f32)
    for m in range(4):
        for copy in copies[m]:
            copy.wait()
        for k in range(4):
            for group in range(groups):
                at = (m * groups + group) * 8
                re = sides_ref[2 * k, at : at + 8, :]
                im = sides_ref[2 * k + 1, at : at + 8, :]
                wr = real_ref[m, group * 4 + k]
                wi = imag_ref[m, group * 4 + k]
                real[m] = real[m] + (re * wr - im * wi)
                imag[m] = imag[m] + (re * wi + im * wr)
    hi, lo = split(jnp.concatenate(real + imag, axis=0))
    placed = jnp.dot(jnp.concatenate([hi, lo], axis=0), order, preferred_element_type=f32)
    placed = placed[0:64] + placed[64:128]
    for block in range(out_ref.shape[0] // 8):
        tiles = [placed[8 * m : 8 * m + 8, block * 128 : (block + 1) * 128] for m in range(8)]
        tiles = swap_lanes(tiles, 16)
        for slot in range(8):
            out_ref[block * 8 + slot] = tiles[slot]


def inverse_z_body(in_ref, hi_ref, lo_ref, conv_ref, out_ref, rows_ref):
    groups = C // 4
    zero = jnp.zeros((8, 128), jnp.float32)
    for group in range(groups):
        tiles = swap_lanes([in_ref[group * 3 + part] for part in range(3)] + [zero], 16)
        for x in range(4):
            rows_ref[32 * group + 8 * x : 32 * group + 8 * x + 8, :] = tiles[x]
    cells = dot(rows_ref[...], hi_ref[...], lo_ref[...])
    for group in range(groups):
        lanes = slice(group * 256, (group + 1) * 256)
        for x in range(4):
            at = 32 * group + 8 * x
            out_ref[x, :, lanes] = gelu(cells[at : at + 8] + conv_ref[x, :, lanes])


def on_chip(value):
    return pltpu.with_memory_space_constraint(value, pltpu.VMEM)


def local_call(body, out_shape, scratch, *operands, keep=True, remote=(), more=()):
    shapes = [jax.ShapeDtypeStruct(getattr(at, "shape", at), getattr(at, "dtype", jnp.float32)) for at in (out_shape, *more)]
    kinds = [pltpu.VMEM if keep else jax.ShapeDtypeStruct] + [pltpu.VMEM] * len(more)
    inside = pl.BlockSpec(memory_space=pltpu.VMEM)
    outside = pl.BlockSpec(memory_space=pltpu.HBM)
    results = pl.pallas_call(
        body,
        out_shape=[kind(at.shape, at.dtype) for kind, at in zip(kinds, shapes)],
        in_specs=[outside if at in remote else inside for at in range(len(operands))],
        out_specs=[inside] * len(shapes),
        scratch_shapes=scratch,
        compiler_params=pltpu.CompilerParams(vmem_limit_bytes=(62 if remote else 24) << 20),
    )(*operands)
    return results if more else results[0]


def complex_product(spec, table, real, imag):
    cosine = jnp.asarray(table.real.astype(np.float32))
    sine = jnp.asarray(table.imag.astype(np.float32))

    def product(left, right):
        return jnp.einsum(spec, left, right, precision=highest)

    return (
        product(cosine, real) - product(sine, imag),
        product(cosine, imag) + product(sine, real),
    )


def transform(wave_x, wave_y, parts, split_to):
    a, b, y, _, x, _, _ = parts.shape
    shaped = jnp.transpose(parts, (3, 0, 4, 1, 2, 5, 6)).reshape(2, a * x, b * y, 4, 4)
    real, imag = complex_product("qy,xykj->xqkj", wave_y, shaped[0], shaped[1])
    real, imag = complex_product("px,xqkj->pqkj", wave_x, real, imag)
    return jnp.stack([real, imag]).reshape((2,) + split_to + (4, 4))


def on_device(state_field, conv_first, conv_second, spec_real, spec_imag):
    rows_here, cols_here = state_field.shape[:2]
    kept_x, kept_y = spec_real.shape[:2]
    count_x, count_y = lax.axis_size("gx"), lax.axis_size("gy")
    devices = count_x * count_y
    total_x, total_y = rows_here * count_x, cols_here * count_y
    groups, thirds = C // 4, MZ // 4
    owners = groups * thirds
    if (rows_here, cols_here) != (4, 8) or owners > devices:
        raise ValueError("unsupported block")
    both = ("gx", "gy")
    row_start = lax.axis_index("gx") * rows_here
    col_start = lax.axis_index("gy") * cols_here
    f32 = jnp.float32

    wave_z = dft_wave(np.arange(MZ), Z, -1.0).reshape(thirds, 4, Z)
    wave_z = np.concatenate([wave_z, np.zeros((1, 4, Z))])
    parts_z = np.stack([wave_z.real, wave_z.imag])
    forward_z = np.einsum("egrz,ck->czegkr", parts_z, np.eye(4)).reshape(4 * Z, 128)
    gains = np.where(np.arange(16) == 0, 1.0, 2.0).reshape(4, 4) / (total_x * total_y * Z)
    inverse_z = np.einsum("egrz,gr,ck->egcrkz", parts_z, gains, np.eye(4)).reshape(128, 4 * Z)
    forward_x = dft_wave(mode_freqs(MX, total_x), total_x, -1.0)
    forward_y = dft_wave(mode_freqs(MY, total_y), total_y, -1.0)
    inverse_x, inverse_y = np.conj(forward_x).T, np.conj(forward_y).T

    def trade(block):
        return lax.all_to_all(block, both, 0, 0, tiled=True)

    def shift(block, axis, ahead):
        steps = range(lax.axis_size(axis) - 1)
        return lax.ppermute(block, axis, [(i, i + 1) if ahead else (i + 1, i) for i in steps])

    fast = (count_x, count_y, kept_x, kept_y) == (8, 4, 4, 8)

    edge, side = (2, cols_here, C * Z), (rows_here, 2, C * Z)
    lines = plane_table(line_table(forward_x, count_x, kept_x, count_x, rows_here), forward_y)
    columns, near, far, first, last, lines = local_call(
        forward_z_body,
        (devices, 8, 128),
        [
            pltpu.VMEM((rows_here, cols_here, C * Z), f32),
            pltpu.VMEM((2, 4 * Z, 128), BF),
            pltpu.SemaphoreType.DMA((3,)),
        ],
        state_field,
        np.stack(halves(forward_z)),
        lines,
        keep=False,
        remote=(0, 1, 2),
        more=(edge, edge, side, side, lines),
    )
    columns = trade(columns)
    ends = range(1, count_x - 1)
    near = lax.ppermute(near, "gx", [(i, i ^ 1) for i in range(count_x) if i ^ 1 < count_x])
    far = lax.ppermute(far, "gx", [(i, (i + 1 ^ 1) - 1) for i in ends])

    if fast:
        modes = local_call(
            plane_body,
            (devices, 8, 128),
            [pltpu.VMEM((256, 128), f32)],
            on_chip(columns),
            on_chip(lines),
            keep=False,
        )
    else:
        parts = columns.reshape(count_x, count_y, cols_here, 2, rows_here, 4, 4)
        modes = transform(forward_x, forward_y, parts, (count_x, kept_x, count_y, kept_y))
        modes = jnp.transpose(modes, (1, 3, 4, 0, 2, 5, 6))
        modes = modes.reshape(devices, kept_y, 2 * kept_x * 16)
    modes = trade(modes)
    odd = lax.axis_index("gx") % 2 == 1

    def framed(middle, low):
        pair = near[:, low : low + 2], far[:, low : low + 2]
        top, bottom = jnp.where(odd, pair[0], pair[1]), jnp.where(odd, pair[1], pair[0])
        return jnp.concatenate([top, middle, bottom], axis=0)

    last, first = framed(last, cols_here - 2), framed(first, 0)
    left, right = shift(last, "gy", True), shift(first, "gy", False)
    places = jnp.arange(128, dtype=jnp.int32)[None, :] + 2
    cell_x = row_start - 2 + places // 16
    cell_y = col_start - 2 + places % 16
    inside = (cell_x >= 0) & (cell_x < total_x) & (cell_y >= 0) & (cell_y < total_y)
    mask = inside.astype(f32)

    if fast:
        mixed = local_call(
            mix_body,
            (devices, 8, 128),
            [pltpu.VMEM((32 * groups, 128), f32)]
            + [pltpu.VMEM((kept_x, C, kept_y, MZ * C), f32)] * 2
            + [pltpu.VMEM((8, 32 * groups, MZ * C), f32)]
            + [pltpu.SemaphoreType.DMA((4, 2))],
            on_chip(modes),
            *[
                jnp.transpose(spec, (0, 2, 1, 3))
                for spec in (spec_real, spec_imag)
            ],
            keep=False,
            remote=(1, 2),
        )
    else:
        modes = modes[:owners].reshape(groups, thirds, kept_y, 2, kept_x, 4, 4)
        modes = jnp.transpose(modes, (3, 4, 2, 0, 5, 1, 6))
        modes = modes.reshape(2, kept_x, kept_y, C, MZ)
        weight_real = spec_real.reshape(kept_x, kept_y, C, MZ, C)
        weight_imag = spec_imag.reshape(kept_x, kept_y, C, MZ, C)

        def product(left, right):
            return jnp.einsum("abik,abiko->abok", left, right, precision=highest)

        mixed = jnp.stack(
            [
                product(modes[0], weight_real) - product(modes[1], weight_imag),
                product(modes[0], weight_imag) + product(modes[1], weight_real),
            ]
        ).reshape(2, kept_x, kept_y, groups, 4, thirds, 4)
        mixed = jnp.transpose(mixed, (3, 5, 2, 0, 1, 4, 6))
        mixed = mixed.reshape(owners, kept_y, 2 * kept_x * 16)
        mixed = jnp.pad(mixed, ((0, devices - owners), (0, 0), (0, 0)))
    mixed = trade(mixed)
    filters = [pltpu.VMEM((9 * BLOCK, DEPTH), f32)] + [pltpu.VMEM((9 * BLOCK, DEPTH), BF)] * 2
    hidden, rest = local_call(
        first_conv_body,
        (TOP + EARLY, 128),
        [
            pltpu.VMEM((8, 16, C * Z), f32),
            pltpu.VMEM((ROWS, 128), f32),
            pltpu.VMEM((ROWS + 2 * TOP, 128), f32),
        ]
        + filters,
        state_field,
        near,
        far,
        left,
        right,
        conv_first,
        mask,
        more=((ROWS + 2 * TOP - EARLY, 128),),
    )

    if fast:
        back = local_call(
            plane_body,
            (devices, 8, 128),
            [pltpu.VMEM((256, 128), f32)],
            on_chip(mixed),
            plane_table(line_table(inverse_x, count_x, rows_here, count_x, kept_x), inverse_y),
            keep=False,
        )
    else:
        parts = mixed.reshape(count_x, count_y, kept_y, 2, kept_x, 4, 4)
        back = transform(inverse_x, inverse_y, parts, (count_x, rows_here, count_y, cols_here))
        back = jnp.transpose(back, (1, 3, 4, 0, 2, 5, 6)).reshape(devices, 8, 128)
    back = trade(back)
    conv_out = local_call(
        second_conv_body,
        (rows_here, cols_here, C * Z),
        [
            pltpu.VMEM((PACKED, 128), BF),
            pltpu.VMEM((PACKED, 128), BF),
            pltpu.VMEM((HALF, 128), f32),
            pltpu.VMEM((2, 64, 128), f32),
            pltpu.VMEM((ROWS - EARLY, 128), f32),
        ]
        + filters,
        on_chip(hidden),
        on_chip(rest),
        mask,
        conv_first,
        conv_second,
    )
    return local_call(
        inverse_z_body,
        (rows_here, cols_here, C * Z),
        [pltpu.VMEM((32 * groups, 128), f32)],
        on_chip(back),
        *halves(inverse_z),
        on_chip(conv_out),
        keep=False,
    )


def solution(mesh):
    in_specs = (P("gx", "gy", None), P(), P(), P("gx", "gy", None, None), P("gx", "gy", None, None))
    out_specs = P("gx", "gy", None)
    return jax.shard_map(on_device, mesh=mesh, in_specs=in_specs, out_specs=out_specs, check_vma=False)
```

```python
import numpy as np
import jax
import jax.numpy as jnp
from jax import lax
from jax.experimental import pallas as pl
from jax.experimental.pallas import tpu as pltpu
from jax.sharding import PartitionSpec as P


C = 36
Z = 64
MX = 16
MY = 16
MZ = 12
BF = jnp.bfloat16
highest = lax.Precision.HIGHEST


def gelu(x):
    return 0.5 * x * (1.0 + lax.erf(x * 0.7071067811865476))


def split(x):
    hi = x.astype(BF)
    return hi, (x - hi.astype(jnp.float32)).astype(BF)


STEP = 4
TOP = 40
DEPTH = 224
ROWS = Z * C
BLOCK = STEP * C
LATE = 2
EARLY = ROWS - LATE * 2 * BLOCK


def load_filters(filter_ref, wide_ref, hi_ref, lo_ref):
    wide_ref[...] = jnp.zeros_like(wide_ref)
    for s in range(9):
        taps = filter_ref[s // 3, s % 3]
        for z in range(STEP):
            at = s * BLOCK + z * C
            lane = TOP - C + C * z
            wide_ref[at : at + C, lane : lane + 3 * C] = taps
    hi_ref[...], lo_ref[...] = split(wide_ref[...])


def convolve(data_ref, hi_ref, lo_ref, store, pairs):
    f32 = jnp.float32

    def step(g, carry):
        at = pl.multiple_of(g * 2 * BLOCK, 8)
        window = jnp.concatenate(
            [data_ref[pl.ds(pl.multiple_of(at + h * BLOCK, 8), DEPTH), :] for h in range(2)], axis=1
        )
        data_hi, data_lo = split(window)
        total = None
        for s in range(9):
            hi = hi_ref[s * BLOCK : (s + 1) * BLOCK, :]
            lo = lo_ref[s * BLOCK : (s + 1) * BLOCK, :]
            part = jnp.dot(hi, data_hi, preferred_element_type=f32) + (
                jnp.dot(lo, data_hi, preferred_element_type=f32)
                + jnp.dot(hi, data_lo, preferred_element_type=f32)
            )
            halves = [part[:, :128], part[:, 128:]]
            shift = (s // 3 - 1) * 16 + s % 3 - 1
            if shift:
                halves = [pltpu.roll(half, -shift % 128, 1) for half in halves]
            total = halves if total is None else [u + v for u, v in zip(total, halves)]
        for h in range(2):
            store(pl.multiple_of(at + h * BLOCK, 8), total[h])
        return carry

    lax.fori_loop(0, pairs, step, 0, unroll=2)


def odd_row():
    return (lax.axis_index("gx") & 1) == 1


def first_conv_body(
    cells_ref, near_ref, far_ref, left_ref, right_ref, filter_ref, mask_ref,
    out_ref, tail_ref, frame_ref, turn_ref, data_ref, wide_ref, hi_ref, lo_ref,
):
    f32 = jnp.float32
    frame_ref[:, 8:16, :] = jnp.zeros((8, 8, C * Z), f32)
    frame_ref[2:6, 0:8, :] = cells_ref[...]

    @pl.when(odd_row())
    def _():
        frame_ref[0:2, 0:8, :] = near_ref[...]
        frame_ref[6:8, 0:8, :] = far_ref[...]

    @pl.when(jnp.logical_not(odd_row()))
    def _():
        frame_ref[0:2, 0:8, :] = far_ref[...]
        frame_ref[6:8, 0:8, :] = near_ref[...]

    for x in range(8):
        frame_ref[x, 8:10, :] = right_ref[x]
        frame_ref[(x + 7) % 8, 14:16, :] = left_ref[x]
    data_ref[0:TOP, :] = jnp.zeros((TOP, 128), f32)
    data_ref[TOP + ROWS :, :] = jnp.zeros((TOP, 128), f32)
    for j in range(C * Z // 128):
        lanes = slice(j * 128, (j + 1) * 128)
        turn_ref[lanes, :] = frame_ref[:, :, lanes].reshape(128, 128).T
    for z in range(Z):
        data_ref[TOP + z * C : TOP + (z + 1) * C, :] = turn_ref[pl.ds(z, C, stride=Z), :]
    load_filters(filter_ref, wide_ref, hi_ref, lo_ref)
    mask = mask_ref[0:1, :]

    def store(at, total):
        turn_ref[pl.ds(at, BLOCK), :] = gelu(total) * mask

    tail_ref[...] = data_ref[EARLY:, :]
    convolve(data_ref, hi_ref, lo_ref, store, EARLY // (2 * BLOCK))
    out_ref[0:TOP, :] = jnp.zeros((TOP, 128), f32)
    out_ref[TOP:, :] = turn_ref[0:EARLY, :]


HALF = ROWS // 2
PACKED = HALF + 2 * TOP


def second_conv_body(
    data_ref, tail_ref, mask_ref, first_ref, filter_ref, out_ref,
    pack_hi_ref, pack_lo_ref, turn_ref, merge_ref, late_ref, wide_ref, hi_ref, lo_ref,
):
    f32 = jnp.float32
    mask = mask_ref[0:1, :]

    def store(at, total):
        late_ref[pl.ds(at, BLOCK), :] = gelu(total) * mask

    load_filters(first_ref, wide_ref, hi_ref, lo_ref)
    convolve(tail_ref, hi_ref, lo_ref, store, LATE)
    load_filters(filter_ref, wide_ref, hi_ref, lo_ref)
    source = lax.broadcasted_iota(jnp.int32, (256, 128), 0)
    target = lax.broadcasted_iota(jnp.int32, (1, 128), 1)
    place = target & 63
    line = jnp.floor((place.astype(f32) + 0.5) * 0.1).astype(jnp.int32)
    wanted = (target >= 64).astype(jnp.int32) * 128 + 16 * (line + 1) + place - 10 * line - 1
    wanted = jnp.where(place < 60, wanted, -1)
    select = jnp.where(source == wanted, 1.0, 0.0).astype(BF)
    upper = [data_ref[HALF : TOP + EARLY, :], late_ref[...], jnp.zeros((TOP, 128), f32)]
    whole = jnp.concatenate([data_ref[0:PACKED, :], jnp.concatenate(upper, axis=0)], axis=1)
    for part, held_ref in zip(split(whole), (pack_hi_ref, pack_lo_ref)):
        held_ref[...] = jnp.dot(part, select, preferred_element_type=f32).astype(BF)

    def step(g, carry):
        at = pl.multiple_of(g * BLOCK, 16)
        later = pl.multiple_of(at + HALF // 2, 16)
        data_hi, data_lo = [
            jnp.concatenate([held[pl.ds(at, DEPTH), :], held[pl.ds(later, DEPTH), :]], axis=1)
            for held in (pack_hi_ref, pack_lo_ref)
        ]
        total = None
        for s in range(9):
            hi = hi_ref[s * BLOCK : (s + 1) * BLOCK, :]
            lo = lo_ref[s * BLOCK : (s + 1) * BLOCK, :]
            part = jnp.dot(hi, data_hi, preferred_element_type=f32) + (
                jnp.dot(lo, data_hi, preferred_element_type=f32)
                + jnp.dot(hi, data_lo, preferred_element_type=f32)
            )
            sides = [part[:, :128], part[:, 128:]]
            shift = (s // 3 - 1) * 10 + s % 3 - 1
            if shift:
                sides = [pltpu.roll(side, -shift % 128, 1) for side in sides]
            total = sides if total is None else [u + v for u, v in zip(total, sides)]
        turn_ref[pl.ds(at, BLOCK), :] = total[0]
        turn_ref[pl.ds(later, BLOCK), :] = total[1]
        return carry

    lax.fori_loop(0, Z // (4 * STEP), step, 0, unroll=2)
    quarter = lax.broadcasted_iota(jnp.int32, (64, 128), 1) >> 5
    for four in range(C // 4):
        pieces = [turn_ref[pl.ds(4 * four + e, Z // 2, stride=C), :] for e in range(4)]
        turned = jnp.concatenate(pieces, axis=0).T
        early, late = turned[:64], turned[64:]
        for pair in range(2):
            turns = ((0, 32, 32, 64), (64, 96, 96, 0))[pair]
            parts = [
                pltpu.roll(side, turn, 1) if turn else side
                for side, turn in zip((early, late, early, late), turns)
            ]
            merge_ref[pair] = jnp.where(
                quarter < 2,
                jnp.where(quarter < 1, parts[0], parts[1]),
                jnp.where(quarter < 3, parts[2], parts[3]),
            )
            at = (2 * four + pair) * 128
            for x in range(4):
                out_ref[x, :, at : at + 128] = merge_ref[pair, 10 * x + 11 : 10 * x + 19, :]


def dft_wave(freqs, length, sign):
    angle = sign * 2.0 * np.pi * np.outer(freqs, np.arange(length)) / length
    return np.cos(angle) + 1j * np.sin(angle)


def mode_freqs(kept, length):
    places = np.arange(2 * kept)
    return np.where(places < kept, places, places + length - 2 * kept)


def halves(table):
    hi = table.astype(BF)
    lo = (table - hi.astype(np.float64)).astype(BF)
    return hi, lo


def line_table(wave, outer_to, inner_to, outer, inner):
    shaped = wave.reshape(outer_to, inner_to, outer, inner)
    turned = np.stack([shaped, shaped * 1j])
    parts = np.stack([turned.real, turned.imag])
    table = np.einsum("crAmal,uv->rlaucmAv", parts, np.eye(2))
    return table.reshape(4 * inner * outer, 4 * inner_to * outer_to)


def plane_table(lines, wave):
    cross = np.concatenate([wave.real, wave.imag])
    cross = np.pad(cross, ((0, 0), (0, lines.shape[1] - cross.shape[1])))
    return np.stack(halves(np.concatenate([lines, cross])))


def dot(left, right_hi, right_lo):
    f32 = jnp.float32
    hi, lo = split(left)
    return jnp.dot(hi, right_hi, preferred_element_type=f32) + (
        jnp.dot(lo, right_hi, preferred_element_type=f32)
        + jnp.dot(hi, right_lo, preferred_element_type=f32)
    )


def swap_lanes(tiles, low):
    tiles = list(tiles)
    lane = lax.broadcasted_iota(jnp.int32, (8, 128), 1)
    bit = 1
    while bit < len(tiles):
        width = low * bit
        upper = (lane & width) != 0
        for at in range(len(tiles)):
            if at & bit == 0:
                first, second = tiles[at], tiles[at | bit]
                tiles[at] = jnp.where(upper, pltpu.roll(second, width, 1), first)
                tiles[at | bit] = jnp.where(upper, second, pltpu.roll(first, 128 - width, 1))
        bit *= 2
    return tiles


def forward_z_body(
    field_ref, waves_ref, lines_ref, out_ref, near_ref, far_ref, first_ref, last_ref, held_ref,
    cells_ref, table_ref, sems,
):
    groups = C // 4
    copies = [
        pltpu.make_async_copy(field_ref, cells_ref, sems.at[0]),
        pltpu.make_async_copy(waves_ref, table_ref, sems.at[1]),
    ]
    later = pltpu.make_async_copy(lines_ref, held_ref, sems.at[2])
    for copy in copies:
        copy.start()
    later.start()
    for copy in copies:
        copy.wait()
    rows = cells_ref.shape[0]
    cols = cells_ref.shape[1]
    first_ref[...] = cells_ref[:, 0:2, :]
    last_ref[...] = cells_ref[:, cols - 2 : cols, :]

    @pl.when(odd_row())
    def _():
        near_ref[...] = cells_ref[0:2]
        far_ref[...] = cells_ref[rows - 2 : rows]

    @pl.when(jnp.logical_not(odd_row()))
    def _():
        near_ref[...] = cells_ref[rows - 2 : rows]
        far_ref[...] = cells_ref[0:2]

    stacked = jnp.concatenate(
        [cells_ref[:, :, g * 256 : (g + 1) * 256].reshape(32, 256) for g in range(groups)], axis=0
    )
    waves = dot(stacked, table_ref[0], table_ref[1])
    for group in range(groups):
        at = 32 * group
        tiles = swap_lanes([waves[at + 8 * x : at + 8 * x + 8] for x in range(4)], 16)
        for part in range(3):
            out_ref[group * 3 + part] = tiles[part]
    for spare in range(3 * groups, out_ref.shape[0]):
        out_ref[spare] = jnp.zeros((8, 128), jnp.float32)
    later.wait()


def plane_body(in_ref, table_ref, out_ref, rows_ref):
    f32 = jnp.float32
    outer, inner = 8, 4
    for b in range(inner):
        tiles = swap_lanes([in_ref[a * inner + b] for a in range(outer)], 2)
        for g in range(8):
            rows_ref[g * 32 + b * 8 : g * 32 + b * 8 + 8, :] = tiles[g]
    lines = dot(rows_ref[...], table_ref[0, 0:128, :], table_ref[1, 0:128, :])
    minus = lax.broadcasted_iota(jnp.int32, (32, 128), 1) < 64
    results = []
    cross_hi, cross_lo = table_ref[0, 128:192, 0:32], table_ref[1, 128:192, 0:32]
    for g in range(0, 8, 2):
        part = jnp.concatenate([lines[g * 32 : g * 32 + 32], lines[g * 32 + 32 : g * 32 + 64]], axis=1)
        hi, lo = split(part)
        both = jnp.dot(cross_hi, hi, preferred_element_type=f32) + (
            jnp.dot(cross_lo, hi, preferred_element_type=f32)
            + jnp.dot(cross_hi, lo, preferred_element_type=f32)
        )
        for h in range(2):
            turned = pltpu.roll(both[32:, h * 128 : h * 128 + 128], 64, 1)
            plain = both[:32, h * 128 : h * 128 + 128]
            results.append(jnp.where(minus, plain - turned, plain + turned))
    for b in range(inner):
        tiles = swap_lanes([results[g][b * 8 : b * 8 + 8] for g in range(8)], 2)
        for a in range(outer):
            out_ref[a * inner + b] = tiles[a]


def mode_of(place):
    return jnp.floor((place.astype(jnp.float32) + 0.5) * (1.0 / C)).astype(jnp.int32)


def mix_body(in_ref, real_hbm, imag_hbm, out_ref, left_ref, real_ref, imag_ref, sides_ref, sems):
    f32 = jnp.float32
    groups = C // 4
    copies = [
        [
            pltpu.make_async_copy(source.at[k], held.at[k], sems.at[k, e])
            for e, (source, held) in enumerate(((real_hbm, real_ref), (imag_hbm, imag_ref)))
        ]
        for k in range(4)
    ]
    for pair in copies:
        for copy in pair:
            copy.start()
    width = MZ * C
    lane = lax.broadcasted_iota(jnp.int32, (128, width), 0)
    mode = mode_of(lax.broadcasted_iota(jnp.int32, (1, width), 1))
    table = jnp.where(lane == (mode >> 2) * 16 + (mode & 3), 1.0, 0.0).astype(BF)
    table = jnp.concatenate([table, table], axis=0)
    place = lax.broadcasted_iota(jnp.int32, (width, 1), 0)
    mode = mode_of(place)
    channel = place - mode * C
    column = ((channel >> 2) * 3 + (mode >> 2)) * 16 + (channel & 3) * 4 + (mode & 3)
    slots = lax.broadcasted_iota(jnp.int32, (width, out_ref.shape[0] * 16), 1)
    order = jnp.where(slots == column, 1.0, 0.0).astype(BF)
    zero = jnp.zeros((8, 128), f32)
    for group in range(groups):
        tiles = swap_lanes([in_ref[group * 3 + part] for part in range(3)] + [zero], 16)
        for m in range(4):
            at = (m * groups + group) * 8
            left_ref[at : at + 8, :] = tiles[m]
    left = left_ref[...]
    real = [jnp.zeros((8, MZ * C), f32) for _ in range(4)]
    imag = [jnp.zeros((8, MZ * C), f32) for _ in range(4)]
    for k in range(4):
        for e in range(2):
            turn = -(e * 64 + k * 4) % 128
            hi, lo = split(pltpu.roll(left, turn, 1) if turn else left)
            turned = jnp.concatenate([hi, lo], axis=1)
            sides_ref[2 * k + e] = jnp.dot(turned, table, preferred_element_type=f32)
    for m in range(4):
        for copy in copies[m]:
            copy.wait()
        for k in range(4):
            for group in range(groups):
                at = (m * groups + group) * 8
                re = sides_ref[2 * k, at : at + 8, :]
                im = sides_ref[2 * k + 1, at : at + 8, :]
                wr = real_ref[m, group * 4 + k]
                wi = imag_ref[m, group * 4 + k]
                real[m] = real[m] + (re * wr - im * wi)
                imag[m] = imag[m] + (re * wi + im * wr)
    hi, lo = split(jnp.concatenate(real + imag, axis=0))
    placed = jnp.dot(jnp.concatenate([hi, lo], axis=0), order, preferred_element_type=f32)
    placed = placed[0:64] + placed[64:128]
    for block in range(out_ref.shape[0] // 8):
        tiles = [placed[8 * m : 8 * m + 8, block * 128 : (block + 1) * 128] for m in range(8)]
        tiles = swap_lanes(tiles, 16)
        for slot in range(8):
            out_ref[block * 8 + slot] = tiles[slot]


def inverse_z_body(in_ref, hi_ref, lo_ref, conv_ref, out_ref, rows_ref):
    groups = C // 4
    zero = jnp.zeros((8, 128), jnp.float32)
    for group in range(groups):
        tiles = swap_lanes([in_ref[group * 3 + part] for part in range(3)] + [zero], 16)
        for x in range(4):
            rows_ref[32 * group + 8 * x : 32 * group + 8 * x + 8, :] = tiles[x]
    cells = dot(rows_ref[...], hi_ref[...], lo_ref[...])
    for group in range(groups):
        lanes = slice(group * 256, (group + 1) * 256)
        for x in range(4):
            at = 32 * group + 8 * x
            out_ref[x, :, lanes] = gelu(cells[at : at + 8] + conv_ref[x, :, lanes])


def on_chip(value):
    return pltpu.with_memory_space_constraint(value, pltpu.VMEM)


def local_call(body, out_shape, scratch, *operands, keep=True, remote=(), more=()):
    shapes = [jax.ShapeDtypeStruct(getattr(at, "shape", at), getattr(at, "dtype", jnp.float32)) for at in (out_shape, *more)]
    kinds = [pltpu.VMEM if keep else jax.ShapeDtypeStruct] + [pltpu.VMEM] * len(more)
    inside = pl.BlockSpec(memory_space=pltpu.VMEM)
    outside = pl.BlockSpec(memory_space=pltpu.HBM)
    results = pl.pallas_call(
        body,
        out_shape=[kind(at.shape, at.dtype) for kind, at in zip(kinds, shapes)],
        in_specs=[outside if at in remote else inside for at in range(len(operands))],
        out_specs=[inside] * len(shapes),
        scratch_shapes=scratch,
        compiler_params=pltpu.CompilerParams(vmem_limit_bytes=(62 if remote else 24) << 20),
    )(*operands)
    return results if more else results[0]


def complex_product(spec, table, real, imag):
    cosine = jnp.asarray(table.real.astype(np.float32))
    sine = jnp.asarray(table.imag.astype(np.float32))

    def product(left, right):
        return jnp.einsum(spec, left, right, precision=highest)

    return (
        product(cosine, real) - product(sine, imag),
        product(cosine, imag) + product(sine, real),
    )


def transform(wave_x, wave_y, parts, split_to):
    a, b, y, _, x, _, _ = parts.shape
    shaped = jnp.transpose(parts, (3, 0, 4, 1, 2, 5, 6)).reshape(2, a * x, b * y, 4, 4)
    real, imag = complex_product("qy,xykj->xqkj", wave_y, shaped[0], shaped[1])
    real, imag = complex_product("px,xqkj->pqkj", wave_x, real, imag)
    return jnp.stack([real, imag]).reshape((2,) + split_to + (4, 4))


def on_device(state_field, conv_first, conv_second, spec_real, spec_imag):
    rows_here, cols_here = state_field.shape[:2]
    kept_x, kept_y = spec_real.shape[:2]
    count_x, count_y = lax.axis_size("gx"), lax.axis_size("gy")
    devices = count_x * count_y
    total_x, total_y = rows_here * count_x, cols_here * count_y
    groups, thirds = C // 4, MZ // 4
    owners = groups * thirds
    if (rows_here, cols_here) != (4, 8) or owners > devices:
        raise ValueError("unsupported block")
    both = ("gx", "gy")
    row_start = lax.axis_index("gx") * rows_here
    col_start = lax.axis_index("gy") * cols_here
    f32 = jnp.float32

    wave_z = dft_wave(np.arange(MZ), Z, -1.0).reshape(thirds, 4, Z)
    wave_z = np.concatenate([wave_z, np.zeros((1, 4, Z))])
    parts_z = np.stack([wave_z.real, wave_z.imag])
    forward_z = np.einsum("egrz,ck->czegkr", parts_z, np.eye(4)).reshape(4 * Z, 128)
    gains = np.where(np.arange(16) == 0, 1.0, 2.0).reshape(4, 4) / (total_x * total_y * Z)
    inverse_z = np.einsum("egrz,gr,ck->egcrkz", parts_z, gains, np.eye(4)).reshape(128, 4 * Z)
    forward_x = dft_wave(mode_freqs(MX, total_x), total_x, -1.0)
    forward_y = dft_wave(mode_freqs(MY, total_y), total_y, -1.0)
    inverse_x, inverse_y = np.conj(forward_x).T, np.conj(forward_y).T

    def trade(block):
        return lax.all_to_all(block, both, 0, 0, tiled=True)

    def shift(block, axis, ahead):
        steps = range(lax.axis_size(axis) - 1)
        return lax.ppermute(block, axis, [(i, i + 1) if ahead else (i + 1, i) for i in steps])

    fast = (count_x, count_y, kept_x, kept_y) == (8, 4, 4, 8)

    edge, side = (2, cols_here, C * Z), (rows_here, 2, C * Z)
    lines = plane_table(line_table(forward_x, count_x, kept_x, count_x, rows_here), forward_y)
    columns, near, far, first, last, lines = local_call(
        forward_z_body,
        (devices, 8, 128),
        [
            pltpu.VMEM((rows_here, cols_here, C * Z), f32),
            pltpu.VMEM((2, 4 * Z, 128), BF),
            pltpu.SemaphoreType.DMA((3,)),
        ],
        state_field,
        np.stack(halves(forward_z)),
        lines,
        keep=False,
        remote=(0, 1, 2),
        more=(edge, edge, side, side, lines),
    )
    columns = trade(columns)
    ends = range(1, count_x - 1)
    near = lax.ppermute(near, "gx", [(i, i ^ 1) for i in range(count_x) if i ^ 1 < count_x])
    far = lax.ppermute(far, "gx", [(i, (i + 1 ^ 1) - 1) for i in ends])

    if fast:
        modes = local_call(
            plane_body,
            (devices, 8, 128),
            [pltpu.VMEM((256, 128), f32)],
            on_chip(columns),
            on_chip(lines),
            keep=False,
        )
    else:
        parts = columns.reshape(count_x, count_y, cols_here, 2, rows_here, 4, 4)
        modes = transform(forward_x, forward_y, parts, (count_x, kept_x, count_y, kept_y))
        modes = jnp.transpose(modes, (1, 3, 4, 0, 2, 5, 6))
        modes = modes.reshape(devices, kept_y, 2 * kept_x * 16)
    modes = trade(modes)
    odd = lax.axis_index("gx") % 2 == 1

    def framed(middle, low):
        pair = near[:, low : low + 2], far[:, low : low + 2]
        top, bottom = jnp.where(odd, pair[0], pair[1]), jnp.where(odd, pair[1], pair[0])
        return jnp.concatenate([top, middle, bottom], axis=0)

    last, first = framed(last, cols_here - 2), framed(first, 0)
    left, right = shift(last, "gy", True), shift(first, "gy", False)
    places = jnp.arange(128, dtype=jnp.int32)[None, :] + 2
    cell_x = row_start - 2 + places // 16
    cell_y = col_start - 2 + places % 16
    inside = (cell_x >= 0) & (cell_x < total_x) & (cell_y >= 0) & (cell_y < total_y)
    mask = inside.astype(f32)

    if fast:
        mixed = local_call(
            mix_body,
            (devices, 8, 128),
            [pltpu.VMEM((32 * groups, 128), f32)]
            + [pltpu.VMEM((kept_x, C, kept_y, MZ * C), f32)] * 2
            + [pltpu.VMEM((8, 32 * groups, MZ * C), f32)]
            + [pltpu.SemaphoreType.DMA((4, 2))],
            on_chip(modes),
            *[
                jnp.transpose(spec, (0, 2, 1, 3))
                for spec in (spec_real, spec_imag)
            ],
            keep=False,
            remote=(1, 2),
        )
    else:
        modes = modes[:owners].reshape(groups, thirds, kept_y, 2, kept_x, 4, 4)
        modes = jnp.transpose(modes, (3, 4, 2, 0, 5, 1, 6))
        modes = modes.reshape(2, kept_x, kept_y, C, MZ)
        weight_real = spec_real.reshape(kept_x, kept_y, C, MZ, C)
        weight_imag = spec_imag.reshape(kept_x, kept_y, C, MZ, C)

        def product(left, right):
            return jnp.einsum("abik,abiko->abok", left, right, precision=highest)

        mixed = jnp.stack(
            [
                product(modes[0], weight_real) - product(modes[1], weight_imag),
                product(modes[0], weight_imag) + product(modes[1], weight_real),
            ]
        ).reshape(2, kept_x, kept_y, groups, 4, thirds, 4)
        mixed = jnp.transpose(mixed, (3, 5, 2, 0, 1, 4, 6))
        mixed = mixed.reshape(owners, kept_y, 2 * kept_x * 16)
        mixed = jnp.pad(mixed, ((0, devices - owners), (0, 0), (0, 0)))
    mixed = trade(mixed)
    filters = [pltpu.VMEM((9 * BLOCK, DEPTH), f32)] + [pltpu.VMEM((9 * BLOCK, DEPTH), BF)] * 2
    hidden, rest = local_call(
        first_conv_body,
        (TOP + EARLY, 128),
        [
            pltpu.VMEM((8, 16, C * Z), f32),
            pltpu.VMEM((ROWS, 128), f32),
            pltpu.VMEM((ROWS + 2 * TOP, 128), f32),
        ]
        + filters,
        state_field,
        near,
        far,
        left,
        right,
        conv_first,
        mask,
        more=((ROWS + 2 * TOP - EARLY, 128),),
    )

    if fast:
        back = local_call(
            plane_body,
            (devices, 8, 128),
            [pltpu.VMEM((256, 128), f32)],
            on_chip(mixed),
            plane_table(line_table(inverse_x, count_x, rows_here, count_x, kept_x), inverse_y),
            keep=False,
        )
    else:
        parts = mixed.reshape(count_x, count_y, kept_y, 2, kept_x, 4, 4)
        back = transform(inverse_x, inverse_y, parts, (count_x, rows_here, count_y, cols_here))
        back = jnp.transpose(back, (1, 3, 4, 0, 2, 5, 6)).reshape(devices, 8, 128)
    back = trade(back)
    conv_out = local_call(
        second_conv_body,
        (rows_here, cols_here, C * Z),
        [
            pltpu.VMEM((PACKED, 128), BF),
            pltpu.VMEM((PACKED, 128), BF),
            pltpu.VMEM((HALF, 128), f32),
            pltpu.VMEM((2, 64, 128), f32),
            pltpu.VMEM((ROWS - EARLY, 128), f32),
        ]
        + filters,
        on_chip(hidden),
        on_chip(rest),
        mask,
        conv_first,
        conv_second,
    )
    return local_call(
        inverse_z_body,
        (rows_here, cols_here, C * Z),
        [pltpu.VMEM((32 * groups, 128), f32)],
        on_chip(back),
        *halves(inverse_z),
        on_chip(conv_out),
        keep=False,
    )


def solution(mesh):
    in_specs = (P("gx", "gy", None), P(), P(), P("gx", "gy", None, None), P("gx", "gy", None, None))
    out_specs = P("gx", "gy", None)
    return jax.shard_map(on_device, mesh=mesh, in_specs=in_specs, out_specs=out_specs, check_vma=False)
```
